32 devices in a mesh: dp: 32 (over z, y, x, core).
Axes of the slice: x: 2, y: 2, z: 4, core: 2. Of those that a mesh axis runs over, the one named last changes fastest.
Arguments:
- layer_in: bfloat16 [3, 32768, 512], P(None, 'dp'), may hold values from -6 to 6
- memory: bfloat16 [3, 8192, 512], P(None, 'dp'), may hold values from -6 to 6
- seg_ids: int32 [3, 32, 1024], P(None, 'dp'), may hold values from 0 to 7, never falling along the last dimension, each value on 1 to 256 neighbouring positions
- offsets: int32 [3, 32, 8], P(None, 'dp'), may hold values from 1 to 1024
- cotangent: bfloat16 [3, 32768, 512], P(None, 'dp'), may hold values from -6 to 6
- attn_q: bfloat16 [2, 512, 512], P(None, 'dp'), may hold values from -0.5 to 0.5
- attn_k: bfloat16 [2, 512, 512], P(None, 'dp'), may hold values from -0.25 to 0.25
- attn_v: bfloat16 [2, 512, 512], P(None, 'dp'), may hold values from -0.25 to 0.25
- attn_o: bfloat16 [2, 512, 512], P(None, 'dp'), may hold values from -1 to 1
- w_in: bfloat16 [512, 2048], P('dp'), may hold values from -0.25 to 0.25
- w_out: bfloat16 [2048, 512], P('dp'), may hold values from -0.1875 to 0.1875
- ffn_bias: bfloat16 [2048], P('dp'), may hold values from -3 to 3
- out_bias: bfloat16 [3, 512], P(None, 'dp'), may hold values from -2 to 2
- omega: bfloat16 [3, 512], P(None, 'dp'), may hold values from 0.5 to 2
- ln_gain: bfloat16 [3, 512], P(None, 'dp'), may hold values from 0.25 to 1.75
- ln_bias: bfloat16 [3, 512], P(None, 'dp'), may hold values from -2 to 2
Outputs:
- layer_out: bfloat16 [3, 32768, 512], P(None, 'dp')
- input_grad: bfloat16 [3, 32768, 512], P(None, 'dp')
- memory_grad: bfloat16 [3, 8192, 512], P(None, 'dp')
- grad_q: float32 [2, 512, 512], P(None, 'dp')
- grad_k: float32 [2, 512, 512], P(None, 'dp')
- grad_v: float32 [2, 512, 512], P(None, 'dp')
- grad_o: float32 [2, 512, 512], P(None, 'dp')
- grad_w_in: float32 [512, 2048], P('dp')
- grad_w_out: float32 [2048, 512], P('dp')
- grad_ffn_bias: float32 [2048], P('dp')
- grad_out_bias: float32 [3, 512], P(None, 'dp')
- grad_omega: float32 [3, 512], P(None, 'dp')
- grad_gain: float32 [3, 512], P(None, 'dp')
- grad_shift: float32 [3, 512], P(None, 'dp')
The draws below stay inside these ranges and needn't reach their ends.
Inputs may be any that keep to these rules, and one draw needn't show every extreme that they name: `seg_ids`: within each block of 1024 rows, the continuation that a row belongs to: never falling along the rows, every continuation present with 1 to 256 rows. Read only in blocks of even index. `offsets`: for each continuation, the number of leading prompt positions that it attends to. Read only in blocks of even index.
All inputs are finite; a program needn't handle non-finite values.
Results may differ from the reference program's by a relative error of at most 0.028.
The reference program's roundings to bfloat16 on the way count: a program that leaves them out, or rounds other values in their place, can miss the bound.
Values may be sent and summed in bfloat16 or wider, within the bound.
No kernel may reach another device: no remote copies, remote signals or barrier semaphores. Data moves between devices by JAX's collectives and lax.ppermute only.
A program may use at most 704 MiB of HBM per device.

```python
import math
import jax
import jax.numpy as jnp
import numpy as np
from jax import lax

D = 512
FF = 2048
HEADS = 8
TOK_DEV = 1024
MEM_DEV = 256
CONTS = 8
CONT_MOST = 256
MICRO = 3
TOKENS = 32768
MEMS = 8192
N_DP = 32


def place_ends(values, rng, smallest, high):
    shape = values.shape
    index_at = [jax.random.randint(jax.random.fold_in(rng, axis), (), 0, shape[axis]) for axis in range(len(shape))]
    values = values.at[tuple(index_at)].set(smallest)
    longest = shape.index(max(shape))
    index_at[longest] = (index_at[longest] + 1) % shape[longest]
    return values.at[tuple(index_at)].set(high)


def strengthened(values, rng, source, target, shards_of, factor):
    def block_of(dim):
        return (jnp.arange(values.shape[dim]) // (values.shape[dim] // shards_of)).reshape((-1,) + (1,) * (values.ndim - 1 - dim))

    near = jax.random.permutation(rng, shards_of)[block_of(target)]
    second = (block_of(target) + shards_of // 2) % shards_of
    return jnp.where((block_of(source) == near) | (block_of(source) == second), factor * values, values)


def block_levels(stream_key, dims, shards, smallest, top_value):
    gain, own = 1.0, jax.random.fold_in(stream_key, 6)
    for dim, shards_of in shards:
        heights = jnp.exp(jax.random.uniform(jax.random.fold_in(own, dim), (shards_of,), jnp.float32, smallest / len(shards), top_value / len(shards)))
        gain = gain * jnp.repeat(heights, dims[dim] // shards_of).reshape([-1 if axis == dim else 1 for axis in range(len(dims))])
    return gain


def split_up(count, total, most, slope):
    loads = [(1 << 20) // math.isqrt(grade ** slope) + 1 for grade in range(2, count + 1)]
    rest, holding = total - most - (count - 1), [1] * (count - 1)
    while rest > 0:
        movable = [i for i in range(count - 1) if holding[i] < most]
        mass, left = sum([loads[i] for i in movable]), rest
        for i in movable:
            extra = min(most - holding[i], max(1, left * loads[i] // mass), rest)
            holding[i] = holding[i] + extra
            rest = rest - extra
    return np.array([most] + holding)


def ragged(key, count, total, most, slope):
    if count == 2:
        one = jax.random.randint(key, (), max(1, total - most), min(most, total - 1) + 1)
        return jnp.stack([one, total - one])
    lengths = jnp.asarray(split_up(count, total, most, slope), jnp.int32)
    pairs = (count - 1) // 2
    source_of, receiver = lengths[1:1 + 2 * pairs:2], lengths[2:2 + 2 * pairs:2]
    slack = jnp.minimum(source_of - 1, most - receiver)
    moved = jax.random.randint(jax.random.fold_in(key, 1), (pairs,), 0, 1 << 20) % (slack + 1)
    lengths = lengths.at[1:1 + 2 * pairs:2].set(source_of - moved).at[2:2 + 2 * pairs:2].set(receiver + moved)
    return lengths[jax.random.permutation(jax.random.fold_in(key, 2), count)]


def scatter_about(own_key, dims, spread, most, pieces=(), kind=jnp.bfloat16):
    entries = jax.random.normal(own_key, dims, jnp.float32) * spread
    if len(pieces) > 0:
        entries = block_levels(own_key, dims, pieces, -0.22, 0.18) * entries
    return jnp.clip(entries, min=-most, max=most).astype(kind)


def gaussian_with(stream_key, dims, scale, bound, cuts, heavy, held_as=jnp.bfloat16):
    entries = scale * jax.random.normal(stream_key, dims, jnp.float32)
    if cuts:
        entries = entries * block_levels(stream_key, dims, cuts, -0.22, 0.18)
    return jnp.clip(strengthened(entries, jax.random.fold_in(stream_key, 3), *heavy), -bound, bound).astype(held_as)


def setup_inputs(seed: int = 0) -> dict:
    arg_keys = jax.random.split(jax.random.key(seed), 17)
    layer_in = gaussian_with(arg_keys[0], (MICRO, TOKENS, D), 1.0, 6.0, ((1, 32),), (1, 2, 32, 2.75))
    memory = gaussian_with(arg_keys[1], (MICRO, MEMS, D), 1.0, 6.0, ((1, 32),), (1, 2, 32, 2.75))
    seg_ids = jax.vmap(lambda own: jnp.searchsorted(jnp.cumsum(ragged(own, CONTS, TOK_DEV, CONT_MOST, 2)), jnp.arange(TOK_DEV), side="right"))(jax.random.split(arg_keys[2], MICRO * N_DP)).reshape((MICRO, N_DP, TOK_DEV)).astype(jnp.int32)
    offsets = place_ends(jax.random.randint(arg_keys[3], (MICRO, N_DP, CONTS), 1, TOK_DEV + 1), jax.random.fold_in(arg_keys[3], 1), 1, TOK_DEV).astype(jnp.int32)
    cotangent = gaussian_with(arg_keys[4], (MICRO, TOKENS, D), 1.0, 6.0, ((1, 32),), (1, 2, 32, 2.75))
    attn_q = scatter_about(arg_keys[5], (2, D, D), (D // 4) ** -0.5, 0.5, ((1, 32),))
    attn_k = scatter_about(arg_keys[6], (2, D, D), D ** -0.5, 0.25, ((1, 32),))
    attn_v = scatter_about(arg_keys[7], (2, D, D), D ** -0.5, 0.25, ((1, 32),))
    attn_o = scatter_about(arg_keys[8], (2, D, D), (D // 16) ** -0.5, 1.0, ((1, 32),))
    w_in = scatter_about(arg_keys[9], (D, FF), D ** -0.5, 0.25, ((0, 32),))
    w_out = scatter_about(arg_keys[10], (FF, D), (FF // 2) ** -0.5, 0.1875, ((0, 32),))
    ffn_bias = scatter_about(arg_keys[11], (FF,), 0.5, 3.0, ((0, 32),))
    out_bias = scatter_about(arg_keys[12], (3, D), 0.3, 2.0, ((1, 32),))
    omega = jnp.clip(jnp.exp(math.log(2.0) - 1.3862944 * jax.random.uniform(arg_keys[13], (3, D), jnp.float32) ** block_levels(arg_keys[13], (3, D), ((1, 32),), -0.2, 0.2)), 0.5, 2.0).astype(jnp.bfloat16)
    ln_gain = jnp.clip(1.0 + 0.15 * jax.random.normal(arg_keys[14], (3, D), jnp.float32), 0.25, 1.75).astype(jnp.bfloat16)
    ln_bias = scatter_about(arg_keys[15], (3, D), 0.3, 2.0, ((1, 32),))
    return dict(layer_in=layer_in, memory=memory, seg_ids=seg_ids, offsets=offsets, cotangent=cotangent, attn_q=attn_q, attn_k=attn_k, attn_v=attn_v, attn_o=attn_o, w_in=w_in, w_out=w_out, ffn_bias=ffn_bias, out_bias=out_bias, omega=omega, ln_gain=ln_gain, ln_bias=ln_bias)


@jax.custom_vjp
def low(v):
    return lax.optimization_barrier(v.astype(jnp.bfloat16)).astype(jnp.float32)

@jax.custom_vjp
def low_back(v):
    return v

def low_keep(v):
    return (low(v), None)

def low_pass(kept, grad):
    return (grad,)

def back_keep(v):
    return (v, None)

def back_low(kept, grad):
    return (low(grad),)
low.defvjp(low_keep, low_pass)
low_back.defvjp(back_keep, back_low)
EPS = 1e-05
NEG = -1e+30
HIGH = lax.Precision.HIGHEST

def product(left, right):
    return jnp.dot(left, right, precision=HIGH)

def smooth_gate(values):
    return jax.nn.gelu(values, approximate=True)

def layer_norm(values, norm_gain, norm_shift):
    row_mean = lax.optimization_barrier(jnp.mean(values, axis=-1, keepdims=True))
    centred = values - row_mean
    inv_std = lax.rsqrt(lax.optimization_barrier(jnp.mean(centred * centred, axis=-1, keepdims=True)) + EPS)
    return centred * inv_std * norm_gain + norm_shift

def attention(queries, key_rows, value_rows, allowed):
    count_q = queries.shape[0]
    head_size = queries.shape[1] // HEADS
    split_q = queries.reshape(count_q, HEADS, head_size)
    split_k = key_rows.reshape(key_rows.shape[0], HEADS, head_size)
    split_v = value_rows.reshape(value_rows.shape[0], HEADS, head_size)
    scores = low_back(jnp.einsum('qhd,khd->hqk', split_q, split_k, precision=HIGH) * head_size ** (-0.5))
    if allowed is not None:
        scores = jnp.where(allowed[None], scores, NEG)
    prob_rows = jax.nn.softmax(scores, axis=-1)
    mixed = jnp.einsum('hqk,khd->qhd', low(prob_rows), split_v, precision=HIGH)
    return low_back(low(mixed.reshape(count_q, -1)))

def group_forward(params, group_rows, mem_rows, seg_row, off_row):
    w_query, w_key, w_value, w_outp, w_first, w_second, bias_ffn, bias_out, omega_res, gains, shifts = params
    half = group_rows.shape[0] // 2
    places = jnp.arange(half, dtype=jnp.int32)
    cont_index = jnp.arange(off_row.shape[0], dtype=jnp.int32)
    reach = lax.optimization_barrier(jnp.sum(jnp.where(seg_row[:, None] == cont_index[None, :], off_row[None, :], 0), axis=1))
    causal = places[None, :] <= places[:, None]
    upper = jnp.concatenate([causal, jnp.zeros((half, half), jnp.bool_)], axis=1)
    lower = jnp.concatenate([places[None, :] < reach[:, None], causal & (seg_row[None, :] == seg_row[:, None])], axis=1)
    allowed = jnp.concatenate([upper, lower], axis=0)
    self_q = low_back(low(product(group_rows, w_query[0])))
    self_k = low_back(low(product(group_rows, w_key[0])))
    self_v = low_back(low(product(group_rows, w_value[0])))
    self_out = attention(self_q, self_k, self_v, allowed)
    branch_a = low_back(product(self_out, w_outp[0]) + bias_out[0])
    first = low(layer_norm(group_rows * omega_res[0] + branch_a, gains[0], shifts[0]))
    cross_q = low_back(low(product(first, w_query[1])))
    mem_k = low_back(low(product(mem_rows, w_key[1])))
    mem_v = low_back(low(product(mem_rows, w_value[1])))
    cross_out = attention(cross_q, mem_k, mem_v, None)
    branch_c = low_back(product(cross_out, w_outp[1]) + bias_out[1])
    second = low(layer_norm(first * omega_res[1] + branch_c, gains[1], shifts[1]))
    hidden_pre = low_back(product(second, w_first) + bias_ffn)
    act = low_back(low(smooth_gate(hidden_pre)))
    branch_f = low_back(product(act, w_second) + bias_out[2])
    return layer_norm(second * omega_res[2] + branch_f, gains[2], shifts[2])

def flip_halves(values, groups):
    return values.reshape(groups, 2, TOK_DEV, D)[:, ::-1].reshape(groups, 2 * TOK_DEV, D)

def reference(layer_in, memory, seg_ids, offsets, cotangent, attn_q, attn_k, attn_v, attn_o, w_in, w_out, ffn_bias, out_bias, omega, ln_gain, ln_bias):
    groups = MICRO * N_DP // 2
    rows_all = flip_halves(layer_in.astype(jnp.float32), groups)
    mem_all = memory.astype(jnp.float32).reshape(groups, 2 * MEM_DEV, D)
    cot_all = flip_halves(cotangent.astype(jnp.float32), groups)
    seg_all = seg_ids.reshape(MICRO, N_DP // 2, 2, TOK_DEV)[:, :, 0].reshape(groups, TOK_DEV).astype(jnp.int32)
    off_all = offsets.reshape(MICRO, N_DP // 2, 2, CONTS)[:, :, 0].reshape(groups, CONTS).astype(jnp.int32)
    params = tuple((p.astype(jnp.float32) for p in (attn_q, attn_k, attn_v, attn_o, w_in, w_out, ffn_bias, out_bias, omega, ln_gain, ln_bias)))

    def whole(rows_in, mem_in, params_in):

        def one_group(item):
            group_rows, mem_rows, seg_row, off_row = item
            return group_forward(params_in, group_rows, mem_rows, seg_row, off_row)
        return lax.map(jax.checkpoint(one_group), (rows_in, mem_in, seg_all, off_all))
    outputs, pullback = jax.vjp(whole, rows_all, mem_all, params)
    grad_rows, grad_mem, grad_params = pullback(cot_all)
    layer_out = flip_halves(outputs, groups).reshape(MICRO, N_DP * TOK_DEV, D).astype(jnp.bfloat16)
    input_grad = flip_halves(grad_rows, groups).reshape(MICRO, N_DP * TOK_DEV, D).astype(jnp.bfloat16)
    memory_grad = grad_mem.reshape(MICRO, N_DP * MEM_DEV, D).astype(jnp.bfloat16)
    return (layer_out, input_grad, memory_grad, grad_params[0], grad_params[1], grad_params[2], grad_params[3], grad_params[4], grad_params[5], grad_params[6], grad_params[7], grad_params[8], grad_params[9], grad_params[10])
```

```python
import functools

import jax
import jax.numpy as jnp
from jax import lax
from jax.experimental import pallas as pl
from jax.experimental.pallas import tpu as pltpu
from jax.sharding import PartitionSpec as P

HEADS = 8
EPS = 1e-05
NEG = -1e30
LANES = 128
VMEM_LIMIT = 56 << 20


def nn(left, right):
    return lax.dot_general(
        left, right, (((1,), (0,)), ((), ())), preferred_element_type=jnp.float32
    )


def nt(left, right):
    return lax.dot_general(
        left, right, (((1,), (1,)), ((), ())), preferred_element_type=jnp.float32
    )


def tn(left, right):
    return lax.dot_general(
        left, right, (((0,), (0,)), ((), ())), preferred_element_type=jnp.float32
    )


def low(values):
    return values.astype(jnp.bfloat16)


def wide(values):
    return values.astype(jnp.float32)


def bit_count(axis):
    return (lax.axis_size(axis) - 1).bit_length()


def from_partner(x, axis, bit):
    return lax.ppermute(x, axis, [(i, i ^ 1 << bit) for i in range(lax.axis_size(axis))])


def prompt_to_continuation(x, axis):
    return lax.ppermute(x, axis, [(i + 1, i) for i in range(0, lax.axis_size(axis), 2)])


def continuation_to_prompt(x, axis):
    return lax.ppermute(x, axis, [(i, i + 1) for i in range(0, lax.axis_size(axis), 2)])


def tree_gather(x, axis):
    bits = bit_count(axis)
    me = lax.axis_index(axis)
    block = x.reshape((1,) * bits + x.shape)
    for bit in list(range(bits - 1, 0, -1)) + [0]:
        dim = bits - 1 - bit
        got = from_partner(block, axis, bit)
        block = jnp.where(
            (me >> bit) & 1 == 1,
            jnp.concatenate([got, block], dim),
            jnp.concatenate([block, got], dim),
        )
    return block.reshape((-1,) + x.shape[1:])


def tree_scatter(arrays, axis):
    bits = bit_count(axis)
    me = lax.axis_index(axis)
    size = lax.axis_size(axis)
    plain = list(range(bits))
    turned = plain[:1] + plain[1:3][::-1] + plain[3:]
    blocks = [
        a.reshape((2,) * bits + (a.shape[0] // size,) + a.shape[1:]) for a in arrays
    ]
    for step in range(bits):
        fresh = []
        for number, block in enumerate(blocks):
            bit = (plain, turned)[number % 2][step]
            dim = bits - 1 - bit
            first = lax.index_in_dim(block, 0, dim, keepdims=True)
            second = lax.index_in_dim(block, 1, dim, keepdims=True)
            upper = (me >> bit) & 1 == 1
            got = from_partner(low(jnp.where(upper, first, second)), axis, bit)
            fresh.append(jnp.where(upper, second, first) + wide(got))
        blocks = fresh
    return [b.reshape((a.shape[0] // size,) + a.shape[1:]) for a, b in zip(arrays, blocks)]


def self_forward_kernel(
    tq, tk, pairs, tiles, q_ref, kp_ref, vp_ref, kl_ref, vl_ref, lim_ref, o_ref, lse_ref, s_ref
):
    micro, tile = pl.program_id(0), pl.program_id(1)
    prefix_tiles = tiles[micro, tile, 0]
    local_first, local_end = tiles[micro, tile, 1], tiles[micro, tile, 2]
    reach, start = lim_ref[0, :, 0:1], lim_ref[0, :, 1:2]
    rows = tile * tq + lax.broadcasted_iota(jnp.int32, (tq, 1), 0)
    lane = lax.broadcasted_iota(jnp.int32, (tq, LANES), 1)
    column = lax.broadcasted_iota(jnp.int32, (tq, tk), 1)
    lse_all = jnp.zeros((tq, LANES), jnp.float32)
    heads = 2 * pairs
    prefix_rows = kp_ref.shape[1]
    half = LANES // 2
    total_pairs = q_ref.shape[2] // LANES

    def prefix_mask(j):
        return column < reach - j * tk

    def local_mask(j):
        return (column <= rows - j * tk) & (column >= start - j * tk)

    for group in range(total_pairs // pairs):
        queries = []
        for h in range(heads):
            p = group * pairs + h // 2
            q = q_ref[0, :, p * LANES : (p + 1) * LANES] * jnp.bfloat16(0.125)
            queries.append(jnp.where((lane >= half) == (h % 2 == 1), q, jnp.bfloat16(0)))

        def score(k_ref, offset, masker, j, tops):
            base = pl.multiple_of(j * tk, tk)
            seen = masker(j)
            out = []
            for h in range(heads):
                p = group * pairs + h // 2
                s = nt(queries[h], k_ref[0, pl.ds(base, tk), p * LANES : (p + 1) * LANES])
                s = jnp.where(seen, s, NEG)
                s_ref[h, :, pl.ds(pl.multiple_of(offset + base, tk), tk)] = s
                top = tops[h]
                for c in range(tk // LANES):
                    top = jnp.maximum(top, s[:, c * LANES : (c + 1) * LANES])
                out.append(top)
            return tuple(out)

        tops = tuple(jnp.full((tq, LANES), NEG, jnp.float32) for _ in range(heads))
        tops = lax.fori_loop(
            0, prefix_tiles, functools.partial(score, kp_ref, 0, prefix_mask), tops
        )
        tops = lax.fori_loop(
            local_first,
            local_end,
            functools.partial(score, kl_ref, prefix_rows, local_mask),
            tops,
        )
        tops = [jnp.max(t, axis=1, keepdims=True) for t in tops]

        def mix(v_ref, offset, j, carry):
            base = pl.multiple_of(j * tk, tk)
            out = []
            for h in range(heads):
                p = group * pairs + h // 2
                e = jnp.exp(
                    s_ref[h, :, pl.ds(pl.multiple_of(offset + base, tk), tk)] - tops[h]
                )
                total, mixed = carry[2 * h], carry[2 * h + 1]
                for c in range(tk // LANES):
                    total = total + e[:, c * LANES : (c + 1) * LANES]
                mixed = mixed + nn(
                    low(e), v_ref[0, pl.ds(base, tk), p * LANES : (p + 1) * LANES]
                )
                out += [total, mixed]
            return tuple(out)

        carry = tuple(jnp.zeros((tq, LANES), jnp.float32) for _ in range(2 * heads))
        carry = lax.fori_loop(0, prefix_tiles, functools.partial(mix, vp_ref, 0), carry)
        carry = lax.fori_loop(
            local_first, local_end, functools.partial(mix, vl_ref, prefix_rows), carry
        )
        for k in range(pairs):
            p = group * pairs + k
            outs = []
            for h in (2 * k, 2 * k + 1):
                total = jnp.sum(carry[2 * h], axis=1, keepdims=True)
                outs.append(carry[2 * h + 1] / total)
                lse_all = jnp.where(lane == 2 * p + h % 2, tops[h] + jnp.log(total), lse_all)
            o_ref[0, :, p * LANES : (p + 1) * LANES] = jnp.where(lane < half, outs[0], outs[1])
    lse_ref[0] = jnp.transpose(lse_all)[0 : lse_ref.shape[1], :]


def self_forward(qkv, far_kv, limits, tiles, tq=256, tk=256, pairs=4):
    micro, rows, width = qkv.shape
    width = width // 3
    whole = (1, rows, width)
    return pl.pallas_call(
        functools.partial(self_forward_kernel, tq, tk, pairs),
        out_shape=(
            jax.ShapeDtypeStruct((micro, rows, width), jnp.float32),
            jax.ShapeDtypeStruct((micro, HEADS, rows), jnp.float32),
        ),
        grid_spec=pltpu.PrefetchScalarGridSpec(
            num_scalar_prefetch=1,
            grid=(micro, rows // tq),
            in_specs=[
                pl.BlockSpec((1, tq, width), lambda m, i, s: (m, i, 0)),
                pl.BlockSpec(whole, lambda m, i, s: (m, 0, 0)),
                pl.BlockSpec(whole, lambda m, i, s: (m, 0, 1)),
                pl.BlockSpec(whole, lambda m, i, s: (m, 0, 1)),
                pl.BlockSpec(whole, lambda m, i, s: (m, 0, 2)),
                pl.BlockSpec((1, tq, 2), lambda m, i, s: (m, i, 0)),
            ],
            out_specs=[
                pl.BlockSpec((1, tq, width), lambda m, i, s: (m, i, 0)),
                pl.BlockSpec((1, HEADS, tq), lambda m, i, s: (m, 0, i)),
            ],
            scratch_shapes=[pltpu.VMEM((2 * pairs, tq, 2 * rows), jnp.float32)],
        ),
        compiler_params=pltpu.CompilerParams(vmem_limit_bytes=VMEM_LIMIT),
        name="self_forward",
    )(tiles, qkv, far_kv, far_kv, qkv, qkv, limits)


def self_backward_kernel(
    tq,
    tk,
    pairs,
    tiles,
    q_ref,
    kp_ref,
    vp_ref,
    kl_ref,
    vl_ref,
    do_ref,
    of_ref,
    lse_ref,
    lim_ref,
    dq_ref,
    dkp_ref,
    dvp_ref,
    dkl_ref,
    dvl_ref,
    sum_kp,
    sum_vp,
    sum_kl,
    sum_vl,
):
    micro = pl.program_id(0)
    row_count = q_ref.shape[1]
    half = LANES // 2
    for ref in (sum_kp, sum_vp, sum_kl, sum_vl):
        ref[...] = jnp.zeros_like(ref)
    lane = lax.broadcasted_iota(jnp.int32, (tq, LANES), 1)
    key_at = lax.broadcasted_iota(jnp.int32, (tk, tq), 0)
    pick_lane = lax.broadcasted_iota(jnp.int32, (8, LANES), 1)
    pick_row = lax.broadcasted_iota(jnp.int32, (8, LANES), 0)
    pick = wide(pick_lane // half == pick_row)
    for i in range(row_count // tq):
        here = slice(i * tq, (i + 1) * tq)
        prefix_tiles = tiles[micro, i, 0]
        local_first, local_end = tiles[micro, i, 1], tiles[micro, i, 2]
        reach, start = lim_ref[0, 0:1, here], lim_ref[0, 1:2, here]
        rows = i * tq + lax.broadcasted_iota(jnp.int32, (1, tq), 1)
        queries, grads, totals, deltas = [], [], [], []
        for k in range(pairs):
            cols = slice(k * LANES, (k + 1) * LANES)
            q = q_ref[0, here, cols] * jnp.bfloat16(0.125)
            do = do_ref[0, here, cols]
            sums = lax.dot_general(
                pick,
                wide(do) * of_ref[0, here, cols],
                (((1,), (1,)), ((), ())),
                preferred_element_type=jnp.float32,
                precision=lax.Precision.HIGHEST,
            )
            for h in range(2):
                mine = (lane >= half) == (h == 1)
                queries.append(jnp.where(mine, q, jnp.bfloat16(0)))
                grads.append(jnp.where(mine, do, jnp.bfloat16(0)))
                totals.append(lse_ref[0, 0, 2 * k + h : 2 * k + h + 1, here])
                deltas.append(sums[h : h + 1, :])

        def body(k_ref, v_ref, sum_k, sum_v, masker, j, dq):
            base = pl.multiple_of(j * tk, tk)
            seen = masker(j)
            out = []
            for k in range(pairs):
                cols = slice(k * LANES, (k + 1) * LANES)
                keys = k_ref[0, pl.ds(base, tk), cols]
                values = v_ref[0, pl.ds(base, tk), cols]
                dv, dk = 0.0, 0.0
                for h in (2 * k, 2 * k + 1):
                    s = jnp.where(seen, nt(keys, queries[h]), NEG)
                    p = jnp.exp(s - totals[h])
                    dp = nt(values, grads[h])
                    dv = dv + nn(low(p), grads[h])
                    ds = low(p * (dp - deltas[h]))
                    dk = dk + nn(ds, queries[h])
                    out.append(dq[h] + tn(ds, keys))
                sum_v[pl.ds(base, tk), cols] += dv
                sum_k[pl.ds(base, tk), cols] += dk
            return tuple(out)

        def prefix_mask(j):
            return key_at < reach - j * tk

        def local_mask(j):
            return (key_at <= rows - j * tk) & (key_at >= start - j * tk)

        dq = tuple(jnp.zeros((tq, LANES), jnp.float32) for _ in range(2 * pairs))
        dq = lax.fori_loop(
            0,
            prefix_tiles,
            functools.partial(body, kp_ref, vp_ref, sum_kp, sum_vp, prefix_mask),
            dq,
        )
        dq = lax.fori_loop(
            local_first,
            local_end,
            functools.partial(body, kl_ref, vl_ref, sum_kl, sum_vl, local_mask),
            dq,
        )
        for k in range(pairs):
            cols = slice(k * LANES, (k + 1) * LANES)
            dq_ref[0, here, cols] = low(jnp.where(lane < half, dq[2 * k], dq[2 * k + 1]) * 0.125)
    dkp_ref[0] = low(sum_kp[...])
    dvp_ref[0] = low(sum_vp[...])
    dkl_ref[0] = sum_kl[...]
    dvl_ref[0] = sum_vl[...]


def self_backward(qkv, far_kv, grad_out, out, lse, limits, tiles, tq=256, tk=256, pairs=2):
    micro, rows, width = qkv.shape
    width = width // 3
    cols = LANES * pairs
    parts = width // cols
    block = (1, rows, cols)
    f32 = jax.ShapeDtypeStruct((micro, rows, width), jnp.float32)
    bf16 = jax.ShapeDtypeStruct((micro, rows, width), jnp.bfloat16)
    return pl.pallas_call(
        functools.partial(self_backward_kernel, tq, tk, pairs),
        out_shape=(bf16, bf16, bf16, f32, f32),
        grid_spec=pltpu.PrefetchScalarGridSpec(
            num_scalar_prefetch=1,
            grid=(micro, parts),
            in_specs=[
                pl.BlockSpec(block, lambda m, i, s: (m, 0, i)),
                pl.BlockSpec(block, lambda m, i, s: (m, 0, i)),
                pl.BlockSpec(block, lambda m, i, s: (m, 0, parts + i)),
                pl.BlockSpec(block, lambda m, i, s: (m, 0, parts + i)),
                pl.BlockSpec(block, lambda m, i, s: (m, 0, 2 * parts + i)),
                pl.BlockSpec(block, lambda m, i, s: (m, 0, i)),
                pl.BlockSpec(block, lambda m, i, s: (m, 0, i)),
                pl.BlockSpec((1, 1, 2 * pairs, rows), lambda m, i, s: (m, i, 0, 0)),
                pl.BlockSpec((1, 2, rows), lambda m, i, s: (m, 0, 0)),
            ],
            out_specs=[pl.BlockSpec(block, lambda m, i, s: (m, 0, i))] * 5,
            scratch_shapes=[pltpu.VMEM((rows, cols), jnp.float32)] * 4,
        ),
        compiler_params=pltpu.CompilerParams(vmem_limit_bytes=VMEM_LIMIT),
        name="self_backward",
    )(
        tiles,
        qkv,
        far_kv,
        far_kv,
        qkv,
        qkv,
        grad_out,
        out,
        lse.reshape(micro, parts, 2 * pairs, rows),
        limits,
    )


def mask_limits(seg, off, is_prompt, tq=256, tk=256):
    micro, rows = seg.shape
    index = jnp.arange(off.shape[1], dtype=jnp.int32)
    own = seg[:, :, None] == index
    count = jnp.sum(own.astype(jnp.int32), axis=1)
    before = jnp.sum(jnp.where(index[:, None] > index[None, :], count[:, None, :], 0), axis=2)
    reach = jnp.sum(jnp.where(own, off[:, None, :], 0), axis=2)
    start = jnp.sum(jnp.where(own, before[:, None, :], 0), axis=2)
    reach = jnp.where(is_prompt, 0, reach)
    start = jnp.where(is_prompt, 0, start)
    tile_count = rows // tq
    most = jnp.max(reach.reshape(micro, tile_count, tq), axis=2)
    least = jnp.min(start.reshape(micro, tile_count, tq), axis=2)
    end = (jnp.arange(tile_count, dtype=jnp.int32) + 1) * tq
    tiles = jnp.stack(
        [
            (most + tk - 1) // tk,
            least // tk,
            jnp.broadcast_to((end + tk - 1) // tk, (micro, tile_count)),
        ],
        axis=2,
    )
    return jnp.stack([reach, start], axis=1), tiles


def smooth_gate(values):
    return jax.nn.gelu(values, approximate=True)


def norm_forward(values, gain, shift):
    mean = jnp.mean(values, axis=-1, keepdims=True)
    centred = values - mean
    inv = lax.rsqrt(jnp.mean(centred * centred, axis=-1, keepdims=True) + EPS)
    normed = centred * inv
    return normed * gain + shift, normed, inv


def norm_backward(grad, normed, inv, gain):
    scaled = grad * gain
    centred = scaled - jnp.mean(scaled, axis=-1, keepdims=True)
    grad_z = inv * (centred - normed * jnp.mean(scaled * normed, axis=-1, keepdims=True))
    rows = tuple(range(grad.ndim - 1))
    return grad_z, jnp.sum(grad * normed, axis=rows), jnp.sum(grad, axis=rows)


def heads_of(values):
    return values.reshape(values.shape[:-1] + (HEADS, values.shape[-1] // HEADS))


def total_tn(left, right):
    return tn(left.reshape(-1, left.shape[-1]), right.reshape(-1, right.shape[-1]))


def flat_nn(left, right):
    return nn(left.reshape(-1, left.shape[-1]), right).reshape(left.shape[:-1] + (right.shape[1],))


def flat_nt(left, right):
    return nt(left.reshape(-1, left.shape[-1]), right).reshape(left.shape[:-1] + (right.shape[0],))


def all_rows(values):
    return jnp.sum(wide(values), axis=(0, 1))


def middle(x, self_out, mem_kv, cot, weights):
    w_o0, w_q1, w_o1, w_in, w_out, ffn_bias, out_bias, omega, gain, shift = weights
    width = x.shape[-1]
    scale = (width // HEADS) ** -0.5
    rows = wide(x)
    self_low = low(self_out)
    h1, n1, i1 = norm_forward(
        rows * omega[0] + (flat_nn(self_low, w_o0) + out_bias[0]), gain[0], shift[0]
    )
    h1 = low(h1)
    cross_q = low(flat_nn(h1, w_q1))
    mem_k, mem_v = heads_of(mem_kv[..., :width]), heads_of(mem_kv[..., width:])
    scores = (
        jnp.einsum(
            "mqhd,mkhd->mhqk", heads_of(cross_q), mem_k, preferred_element_type=jnp.float32
        )
        * scale
    )
    prob = jax.nn.softmax(scores, axis=-1)
    cross = low(
        jnp.einsum("mhqk,mkhd->mqhd", low(prob), mem_v, preferred_element_type=jnp.float32)
    ).reshape(x.shape)
    h2, n2, i2 = norm_forward(
        wide(h1) * omega[1] + (flat_nn(cross, w_o1) + out_bias[1]), gain[1], shift[1]
    )
    h2 = low(h2)
    pre = flat_nn(h2, w_in) + ffn_bias
    act = low(smooth_gate(pre))
    final, n3, i3 = norm_forward(
        wide(h2) * omega[2] + (flat_nn(act, w_out) + out_bias[2]), gain[2], shift[2]
    )
    top = wide(cot)
    dz3, g_gain3, g_shift3 = norm_backward(top, n3, i3, gain[2])
    g_om3 = jnp.sum(dz3 * wide(h2), axis=(0, 1))
    df = low(dz3)
    dact = low(flat_nt(df, w_out))
    dpre = low(jax.vjp(smooth_gate, pre)[1](wide(dact))[0])
    dh2 = flat_nt(dpre, w_in) + dz3 * omega[2]
    dz2, g_gain2, g_shift2 = norm_backward(dh2, n2, i2, gain[1])
    g_om2 = jnp.sum(dz2 * wide(h1), axis=(0, 1))
    dc = low(dz2)
    dco = heads_of(low(flat_nt(dc, w_o1)))
    dprob = jnp.einsum("mqhd,mkhd->mhqk", dco, mem_v, preferred_element_type=jnp.float32)
    ds = low(prob * (dprob - jnp.sum(dprob * prob, axis=-1, keepdims=True)))
    dcq = low(
        jnp.einsum("mhqk,mkhd->mqhd", ds, mem_k, preferred_element_type=jnp.float32) * scale
    ).reshape(x.shape)
    dmk = (
        jnp.einsum(
            "mhqk,mqhd->mkhd", ds, heads_of(cross_q), preferred_element_type=jnp.float32
        )
        * scale
    ).reshape(mem_kv.shape[:2] + (width,))
    dmv = jnp.einsum(
        "mhqk,mqhd->mkhd", low(prob), dco, preferred_element_type=jnp.float32
    ).reshape(mem_kv.shape[:2] + (width,))
    dh1 = flat_nt(dcq, w_q1) + dz2 * omega[1]
    dz1, g_gain1, g_shift1 = norm_backward(dh1, n1, i1, gain[0])
    g_om1 = jnp.sum(dz1 * rows, axis=(0, 1))
    da = low(dz1)
    dso = low(flat_nt(da, w_o0))
    products = (
        total_tn(self_low, da),
        total_tn(h1, dcq),
        total_tn(cross, dc),
        total_tn(h2, dpre),
        total_tn(act, df),
    )
    small = (
        all_rows(dpre),
        jnp.stack([all_rows(da), all_rows(dc), all_rows(df)]),
        jnp.stack([g_om1, g_om2, g_om3]),
        jnp.stack([g_gain1, g_gain2, g_gain3]),
        jnp.stack([g_shift1, g_shift2, g_shift3]),
    )
    return low(final), dso, dz1 * omega[0], dmk, dmv, products, small


def body(
    layer_in,
    memory,
    seg_ids,
    offsets,
    cotangent,
    attn_q,
    attn_k,
    attn_v,
    attn_o,
    w_in,
    w_out,
    ffn_bias,
    out_bias,
    omega,
    ln_gain,
    ln_bias,
):
    axis = "dp"
    is_prompt = lax.axis_index(axis) % 2 == 1
    own_rows = attn_q.shape[1]
    width = attn_q.shape[2]
    hidden = w_in.shape[1]
    mem_rows = memory.shape[1]

    first = tree_gather(jnp.concatenate([attn_q[0], attn_k[0], attn_v[0]], axis=1), axis)
    far_x = prompt_to_continuation(layer_in, axis)
    mem_all = jnp.concatenate([memory, from_partner(memory, axis, 0)], axis=1)
    small = jnp.concatenate(
        [out_bias.T, omega.T, ln_gain.T, ln_bias.T, ffn_bias.reshape(own_rows, -1)], axis=1
    )
    small_cols = small.shape[1]
    rest = lax.all_gather(
        jnp.concatenate(
            [
                attn_o[0],
                attn_q[1],
                attn_o[1],
                attn_k[1],
                attn_v[1],
                w_in,
                w_out.reshape(own_rows, -1),
                jnp.pad(small, ((0, 0), (0, LANES - small_cols))),
            ],
            axis=1,
        ),
        axis,
        axis=0,
        tiled=True,
    )
    w_o0, w_q1, w_o1 = (rest[:, k * width : (k + 1) * width] for k in range(3))
    w_mem = rest[:, 3 * width : 5 * width]
    all_in = rest[:, 5 * width : 5 * width + hidden]
    all_out = rest[:, 5 * width + hidden : 5 * width + 2 * hidden].reshape(hidden, width)
    small = wide(rest[:, 5 * width + 2 * hidden :][:, :small_cols])
    biases, omegas, gains, shifts = (small[:, 3 * k : 3 * k + 3].T for k in range(4))
    all_ffn_bias = small[:, 12:].reshape(hidden)

    limits, tiles = mask_limits(seg_ids[:, 0], offsets[:, 0], is_prompt)
    qkv = low(flat_nn(layer_in, first))
    far_kv = low(flat_nn(far_x, first[:, width:]))
    self_out, lse = self_forward(qkv, far_kv, jnp.swapaxes(limits, 1, 2), tiles)
    mem_kv = low(flat_nn(mem_all, w_mem))
    final, dso, skip, dmk, dmv, products, small_sums = middle(
        layer_in,
        self_out,
        mem_kv,
        cotangent,
        (w_o0, w_q1, w_o1, all_in, all_out, all_ffn_bias, biases, omegas, gains, shifts),
    )
    got_dk = from_partner(low(dmk[:, mem_rows:]), axis, 0)
    got_dv = from_partner(low(dmv[:, mem_rows:]), axis, 0)
    mem_dk = low(dmk[:, :mem_rows] + wide(got_dk))
    mem_dv = low(dmv[:, :mem_rows] + wide(got_dv))
    memory_grad = low(
        flat_nt(mem_dk, w_mem[:, :width]) + flat_nt(mem_dv, w_mem[:, width:])
    )
    g_ffn, g_out, g_om, g_gain, g_shift = small_sums
    small_grad = jnp.concatenate(
        [g_out.T, g_om.T, g_gain.T, g_shift.T, g_ffn.reshape(width, -1)], axis=1
    )
    ready = tree_scatter(
        [
            products[4],
            products[3],
            products[0],
            products[1],
            products[2],
            total_tn(memory, mem_dk),
            total_tn(memory, mem_dv),
            small_grad,
        ],
        axis,
    )
    s_out, s_in, s_o0, s_q1, s_o1, s_k1, s_v1, s_small = ready

    dq, far_dk, far_dv, own_dk, own_dv = self_backward(
        qkv, far_kv, dso, self_out, lse, limits, tiles
    )
    dk = low(own_dk + wide(continuation_to_prompt(far_dk, axis)))
    dv = low(own_dv + wide(continuation_to_prompt(far_dv, axis)))
    s_q0, s_k0, s_v0 = tree_scatter(
        [total_tn(layer_in, dq), total_tn(layer_in, dk), total_tn(layer_in, dv)], axis
    )
    input_grad = low(
        flat_nt(dq, first[:, :width])
        + flat_nt(dk, first[:, width : 2 * width])
        + flat_nt(dv, first[:, 2 * width :])
        + skip
    )
    return (
        final,
        input_grad,
        memory_grad,
        jnp.stack([s_q0, s_q1]),
        jnp.stack([s_k0, s_k1]),
        jnp.stack([s_v0, s_v1]),
        jnp.stack([s_o0, s_o1]),
        s_in,
        s_out,
        s_small[:, 12:].reshape(-1),
        s_small[:, 0:3].T,
        s_small[:, 3:6].T,
        s_small[:, 6:9].T,
        s_small[:, 9:12].T,
    )


def solution(mesh):
    rows = P(None, "dp", None)
    small = P(None, "dp")
    return jax.shard_map(
        body,
        mesh=mesh,
        in_specs=(rows,) * 9 + (P("dp", None), P("dp", None), P("dp"), small, small, small, small),
        out_specs=(rows,) * 7 + (P("dp", None), P("dp", None), P("dp"), small, small, small, small),
        check_vma=False,
    )
```

```python
import functools

import jax
import jax.numpy as jnp
from jax import lax
from jax.experimental import pallas as pl
from jax.experimental.pallas import tpu as pltpu
from jax.sharding import PartitionSpec as P

HEADS = 8
EPS = 1e-05
NEG = -1e30
LANES = 128
VMEM_LIMIT = 56 << 20


def nn(left, right):
    return lax.dot_general(
        left, right, (((1,), (0,)), ((), ())), preferred_element_type=jnp.float32
    )


def nt(left, right):
    return lax.dot_general(
        left, right, (((1,), (1,)), ((), ())), preferred_element_type=jnp.float32
    )


def tn(left, right):
    return lax.dot_general(
        left, right, (((0,), (0,)), ((), ())), preferred_element_type=jnp.float32
    )


def low(values):
    return values.astype(jnp.bfloat16)


def wide(values):
    return values.astype(jnp.float32)


def bit_count(axis):
    return (lax.axis_size(axis) - 1).bit_length()


def from_partner(x, axis, bit):
    return lax.ppermute(x, axis, [(i, i ^ 1 << bit) for i in range(lax.axis_size(axis))])


def prompt_to_continuation(x, axis):
    return lax.ppermute(x, axis, [(i + 1, i) for i in range(0, lax.axis_size(axis), 2)])


def continuation_to_prompt(x, axis):
    return lax.ppermute(x, axis, [(i, i + 1) for i in range(0, lax.axis_size(axis), 2)])


def tree_gather(x, axis):
    bits = bit_count(axis)
    me = lax.axis_index(axis)
    block = x.reshape((1,) * bits + x.shape)
    for bit in list(range(bits - 1, 0, -1)) + [0]:
        dim = bits - 1 - bit
        got = from_partner(block, axis, bit)
        block = jnp.where(
            (me >> bit) & 1 == 1,
            jnp.concatenate([got, block], dim),
            jnp.concatenate([block, got], dim),
        )
    return block.reshape((-1,) + x.shape[1:])


class TreeScatter:
    def __init__(self, arrays, orders, axis):
        self.axis = axis
        self.bits = bit_count(axis)
        self.me = lax.axis_index(axis)
        self.blocks, self.orders, self.steps, self.shapes = [], [], [], []
        self.coming = {}
        self.join(arrays, orders)

    def join(self, arrays, orders):
        size = lax.axis_size(self.axis)
        plain = list(range(self.bits))
        turned = plain[:1] + plain[1:3][::-1] + plain[3:]
        for array, order in zip(arrays, orders):
            own = (array.shape[0] // size,) + array.shape[1:]
            self.blocks.append(array.reshape((2,) * self.bits + own))
            self.orders.append((plain, turned)[order])
            self.steps.append(0)
            self.shapes.append(own)

    def halves(self, number):
        bit = self.orders[number][self.steps[number]]
        dim = self.bits - 1 - bit
        mine = (self.me >> bit) & 1
        block = self.blocks[number]
        keep = lax.dynamic_index_in_dim(block, mine, dim, keepdims=True)
        away = lax.dynamic_index_in_dim(block, 1 - mine, dim, keepdims=True)
        return bit, keep, low(away)

    def send(self, after=None):
        live = [n for n in range(len(self.blocks)) if self.steps[n] < self.bits]
        parts = {n: self.halves(n) for n in live}
        aways = [parts[n][2] for n in live]
        if after is not None:
            after, aways = lax.optimization_barrier((after, aways))
        for n, away in zip(live, aways):
            bit, keep, _ = parts[n]
            self.coming[n] = (keep, from_partner(away, self.axis, bit))
        return after, live

    def receive(self, behind=None):
        for n, (keep, got) in self.coming.items():
            if behind is not None:
                got, _ = lax.optimization_barrier((got, behind))
            self.blocks[n] = wide(keep) + wide(got)
            self.steps[n] += 1
        self.coming = {}

    def finish(self):
        while any(step < self.bits for step in self.steps):
            self.send()
            self.receive()
        return [wide(b.reshape(own)) for b, own in zip(self.blocks, self.shapes)]


def tall_sum(values):
    return jnp.sum(values.reshape(-1, 8, values.shape[1]), axis=0)


def tall_max(values):
    return jnp.max(values.reshape(-1, 8, values.shape[1]), axis=0)


def alone(pair, number):
    half = pair.shape[0] // 2
    blank = jnp.zeros((half, pair.shape[1]), pair.dtype)
    if number == 0:
        return jnp.concatenate([pair[:half], blank], axis=0)
    return jnp.concatenate([blank, pair[half:]], axis=0)


def project_kernel(x_ref, far_ref, w_ref, qt_ref, kv_ref, kvt_ref, fkv_ref, fkvt_ref):
    width = x_ref.shape[2]
    for c in range(3):
        part = slice(c * width, (c + 1) * width)
        here = low(nn(x_ref[0], w_ref[:, part]))
        if c == 0:
            qt_ref[0] = jnp.transpose(here)
            continue
        into = slice((c - 1) * width, c * width)
        kv_ref[0, :, into] = here
        kvt_ref[0, into, :] = jnp.transpose(here)
        there = low(nn(far_ref[0], w_ref[:, part]))
        fkv_ref[0, :, into] = there
        fkvt_ref[0, into, :] = jnp.transpose(there)


def project(x, far, w, block=512):
    micro, rows, width = x.shape
    tall = lambda n: jax.ShapeDtypeStruct((micro, n, rows), jnp.bfloat16)
    long = jax.ShapeDtypeStruct((micro, rows, 2 * width), jnp.bfloat16)
    rows_in = pl.BlockSpec((1, block, width), lambda m, i: (m, i, 0))
    rows_out = pl.BlockSpec((1, block, 2 * width), lambda m, i: (m, i, 0))
    turned = lambda n: pl.BlockSpec((1, n, block), lambda m, i: (m, 0, i))
    return pl.pallas_call(
        project_kernel,
        out_shape=(tall(width), long, tall(2 * width), long, tall(2 * width)),
        grid=(micro, rows // block),
        in_specs=[
            rows_in,
            rows_in,
            pl.BlockSpec(w.shape, lambda m, i: (0, 0), pipeline_mode=pl.Buffered(1)),
        ],
        out_specs=[turned(width), rows_out, turned(2 * width), rows_out, turned(2 * width)],
        compiler_params=pltpu.CompilerParams(vmem_limit_bytes=VMEM_LIMIT),
        cost_estimate=pl.CostEstimate(
            flops=2 * 5 * micro * rows * width * width,
            bytes_accessed=22 * micro * rows * width,
            transcendentals=0,
        ),
        name="project",
    )(x, far, w)


def self_forward_kernel(
    tq, tk, pairs, tiles, qt_ref, kp_ref, kl_ref, vtp_ref, vtl_ref, lim_ref, ot_ref, lse_ref, s_ref
):
    micro, tile = pl.program_id(0), pl.program_id(1)
    prefix_rows = kp_ref.shape[1]
    prefix_tiles = tiles[micro, tile, 0]
    local_first, local_end = tiles[micro, tile, 1], tiles[micro, tile, 2]
    reach, start = lim_ref[0, 0:1, :], lim_ref[0, 1:2, :]
    rows = tile * tq + lax.broadcasted_iota(jnp.int32, (1, tq), 1)
    key_at = lax.broadcasted_iota(jnp.int32, (tk, tq), 0)
    heads = 2 * pairs
    size = LANES // 2

    def prefix_mask(j):
        return key_at < reach - j * tk

    def local_mask(j):
        return (key_at <= rows - j * tk) & (key_at >= start - j * tk)

    for group in range(HEADS // heads):
        queries = []
        for h in range(heads):
            p = group * pairs + h // 2
            pair = qt_ref[0, p * LANES : (p + 1) * LANES, :] * jnp.bfloat16(0.125)
            queries.append(alone(pair, h % 2))

        def score(k_ref, offset, masker, j, tops):
            base = pl.multiple_of(j * tk, tk)
            seen = masker(j)
            out = []
            for h in range(heads):
                p = group * pairs + h // 2
                s = nn(k_ref[0, pl.ds(base, tk), p * LANES : (p + 1) * LANES], queries[h])
                s = jnp.where(seen, s, NEG)
                s_ref[h, pl.ds(pl.multiple_of(offset + base, tk), tk), :] = s
                out.append(jnp.maximum(tops[h], tall_max(s)))
            return tuple(out)

        tops = tuple(jnp.full((8, tq), NEG, jnp.float32) for _ in range(heads))
        tops = lax.fori_loop(
            0, prefix_tiles, functools.partial(score, kp_ref, 0, prefix_mask), tops
        )
        tops = lax.fori_loop(
            local_first,
            local_end,
            functools.partial(score, kl_ref, prefix_rows, local_mask),
            tops,
        )
        tops = [jnp.max(t, axis=0, keepdims=True) for t in tops]

        def mix(vt_ref, offset, j, carry):
            base = pl.multiple_of(j * tk, tk)
            out = []
            for h in range(heads):
                head = group * heads + h
                e = jnp.exp(
                    s_ref[h, pl.ds(pl.multiple_of(offset + base, tk), tk), :] - tops[h]
                )
                total, mixed = carry[2 * h], carry[2 * h + 1]
                out.append(total + tall_sum(e))
                out.append(
                    mixed
                    + nn(vt_ref[0, head * size : (head + 1) * size, pl.ds(base, tk)], low(e))
                )
            return tuple(out)

        carry = (jnp.zeros((8, tq), jnp.float32), jnp.zeros((size, tq), jnp.float32)) * heads
        carry = lax.fori_loop(0, prefix_tiles, functools.partial(mix, vtp_ref, 0), carry)
        carry = lax.fori_loop(
            local_first, local_end, functools.partial(mix, vtl_ref, prefix_rows), carry
        )
        for h in range(heads):
            head = group * heads + h
            total = jnp.sum(carry[2 * h], axis=0, keepdims=True)
            ot_ref[0, head * size : (head + 1) * size, :] = carry[2 * h + 1] / total
            lse_ref[0, head : head + 1, :] = tops[h] + jnp.log(total)


def self_forward(qt, kv, kvt, far_kv, far_kvt, limits, tiles, tq=256, tk=256, pairs=4):
    micro, width, rows = qt.shape
    return pl.pallas_call(
        functools.partial(self_forward_kernel, tq, tk, pairs),
        out_shape=(
            jax.ShapeDtypeStruct((micro, width, rows), jnp.float32),
            jax.ShapeDtypeStruct((micro, HEADS, rows), jnp.float32),
        ),
        grid_spec=pltpu.PrefetchScalarGridSpec(
            num_scalar_prefetch=1,
            grid=(micro, rows // tq),
            in_specs=[
                pl.BlockSpec((1, width, tq), lambda m, i, s: (m, 0, i)),
                pl.BlockSpec((1, rows, width), lambda m, i, s: (m, 0, 0)),
                pl.BlockSpec((1, rows, width), lambda m, i, s: (m, 0, 0)),
                pl.BlockSpec((1, width, rows), lambda m, i, s: (m, 1, 0)),
                pl.BlockSpec((1, width, rows), lambda m, i, s: (m, 1, 0)),
                pl.BlockSpec((1, 2, tq), lambda m, i, s: (m, 0, i)),
            ],
            out_specs=[
                pl.BlockSpec((1, width, tq), lambda m, i, s: (m, 0, i)),
                pl.BlockSpec((1, HEADS, tq), lambda m, i, s: (m, 0, i)),
            ],
            scratch_shapes=[pltpu.VMEM((2 * pairs, 2 * rows, tq), jnp.float32)],
        ),
        compiler_params=pltpu.CompilerParams(vmem_limit_bytes=VMEM_LIMIT),
        cost_estimate=pl.CostEstimate(
            flops=4 * micro * rows * rows * width,
            bytes_accessed=16 * micro * rows * width,
            transcendentals=micro * rows * rows * HEADS,
        ),
        name="self_forward",
    )(tiles, qt, far_kv, kv, far_kvt, kvt, limits)


def self_backward_kernel(
    micro,
    tq,
    tk,
    pairs,
    tiles,
    qt_ref,
    kp_ref,
    vp_ref,
    kl_ref,
    vl_ref,
    ktp_ref,
    ktl_ref,
    dot_ref,
    lse_ref,
    delta_ref,
    lim_ref,
    x_ref,
    far_ref,
    dqt_ref,
    dkp_ref,
    dvp_ref,
    dkl_ref,
    dvl_ref,
    g_ref,
    sum_kp,
    sum_vp,
    sum_kl,
    sum_vl,
    sum_q,
):
    row_count = qt_ref.shape[2]
    size = LANES // 2
    for ref in (sum_kp, sum_vp, sum_kl, sum_vl):
        ref[...] = jnp.zeros_like(ref)
    key_at = lax.broadcasted_iota(jnp.int32, (tk, tq), 0)
    for i in range(row_count // tq):
        here = slice(i * tq, (i + 1) * tq)
        prefix_tiles = tiles[micro, i, 0]
        local_first, local_end = tiles[micro, i, 1], tiles[micro, i, 2]
        reach, start = lim_ref[0, 0:1, here], lim_ref[0, 1:2, here]
        rows = i * tq + lax.broadcasted_iota(jnp.int32, (1, tq), 1)
        queries, grads, totals, deltas = [], [], [], []
        for h in range(2 * pairs):
            part = slice(h // 2 * LANES, (h // 2 + 1) * LANES)
            queries.append(alone(qt_ref[0, part, here] * jnp.bfloat16(0.125), h % 2))
            grads.append(alone(dot_ref[0, part, here], h % 2))
            totals.append(lse_ref[0, 0, h : h + 1, here])
            deltas.append(delta_ref[0, 0, h : h + 1, here])
        sum_q[...] = jnp.zeros_like(sum_q)

        def body(k_ref, v_ref, kt_ref, sum_k, sum_v, masker, j, _):
            base = pl.multiple_of(j * tk, tk)
            seen = masker(j)
            for k in range(pairs):
                cols = slice(k * LANES, (k + 1) * LANES)
                keys = k_ref[0, pl.ds(base, tk), cols]
                values = v_ref[0, pl.ds(base, tk), cols]
                for h in (2 * k, 2 * k + 1):
                    s = jnp.where(seen, nn(keys, queries[h]), NEG)
                    p = jnp.exp(s - totals[h])
                    dp = nn(values, grads[h])
                    sum_v[pl.ds(base, tk), cols] += nt(low(p), grads[h])
                    ds = low(p * (dp - deltas[h]))
                    sum_k[pl.ds(base, tk), cols] += nt(ds, queries[h])
                    part = slice(h * size, (h + 1) * size)
                    sum_q[part, :] += nn(kt_ref[0, part, pl.ds(base, tk)], ds)
            return 0

        def prefix_mask(j):
            return key_at < reach - j * tk

        def local_mask(j):
            return (key_at <= rows - j * tk) & (key_at >= start - j * tk)

        lax.fori_loop(
            0,
            prefix_tiles,
            functools.partial(body, kp_ref, vp_ref, ktp_ref, sum_kp, sum_vp, prefix_mask),
            0,
        )
        lax.fori_loop(
            local_first,
            local_end,
            functools.partial(body, kl_ref, vl_ref, ktl_ref, sum_kl, sum_vl, local_mask),
            0,
        )
        dqt_ref[0, :, here] = low(sum_q[...] * 0.125)
    dkp_ref[0] = low(sum_kp[...])
    dvp_ref[0] = low(sum_vp[...])
    dkl_ref[0] = low(sum_kl[...])
    dvl_ref[0] = low(sum_vl[...])
    width = x_ref.shape[2]
    own, far = jnp.transpose(x_ref[0]), jnp.transpose(far_ref[0])
    g_ref[:, :width] = nt(own, dqt_ref[0])
    g_ref[:, width : 2 * width] = nn(own, dkl_ref[0]) + nn(far, dkp_ref[0])
    g_ref[:, 2 * width :] = nn(own, dvl_ref[0]) + nn(far, dvp_ref[0])


def self_backward(
    number, qt, kv, kvt, far_kv, far_kvt, grad_out, lse, delta, limits, tiles, x, far_x
):
    tq, tk, pairs = 256, 256, HEADS // 2
    micro, width, rows = qt.shape
    tall = pl.BlockSpec((1, width, rows), lambda i, s: (number, 0, 0))
    long = lambda place: pl.BlockSpec((1, rows, width), lambda i, s: (number, 0, place))
    line = pl.BlockSpec((1, 1, HEADS, rows), lambda i, s: (number, 0, 0, 0))
    tall_out = pl.BlockSpec((1, width, rows), lambda i, s: (0, 0, 0))
    long_out = pl.BlockSpec((1, rows, width), lambda i, s: (0, 0, 0))
    bf16 = jax.ShapeDtypeStruct((1, rows, width), jnp.bfloat16)
    return pl.pallas_call(
        functools.partial(self_backward_kernel, number, tq, tk, pairs),
        out_shape=(
            jax.ShapeDtypeStruct((1, width, rows), jnp.bfloat16),
            bf16,
            bf16,
            bf16,
            bf16,
            jax.ShapeDtypeStruct((width, 3 * width), jnp.float32),
        ),
        grid_spec=pltpu.PrefetchScalarGridSpec(
            num_scalar_prefetch=1,
            grid=(1,),
            in_specs=[
                tall,
                long(0),
                long(1),
                long(0),
                long(1),
                tall,
                tall,
                tall,
                line,
                line,
                pl.BlockSpec((1, 2, rows), lambda i, s: (number, 0, 0)),
                long(0),
                long(0),
            ],
            out_specs=[tall_out]
            + [long_out] * 4
            + [pl.BlockSpec((width, 3 * width), lambda i, s: (0, 0))],
            scratch_shapes=[pltpu.VMEM((rows, width), jnp.float32)] * 4
            + [pltpu.VMEM((width, tq), jnp.float32)],
        ),
        compiler_params=pltpu.CompilerParams(vmem_limit_bytes=60 << 20),
        cost_estimate=pl.CostEstimate(
            flops=10 * rows * rows * width,
            bytes_accessed=40 * rows * width,
            transcendentals=rows * rows * HEADS,
        ),
        name="self_backward",
    )(
        tiles,
        qt,
        far_kv,
        far_kv,
        kv,
        kv,
        far_kvt,
        kvt,
        grad_out,
        lse[:, None],
        delta[:, None],
        limits,
        x,
        far_x,
    )


def mask_limits(seg, off, is_prompt, tq=256, tk=256):
    micro, rows = seg.shape
    index = jnp.arange(off.shape[1], dtype=jnp.int32)
    own = seg[:, :, None] == index
    count = jnp.sum(own.astype(jnp.int32), axis=1)
    before = jnp.sum(jnp.where(index[:, None] > index[None, :], count[:, None, :], 0), axis=2)
    reach = jnp.sum(jnp.where(own, off[:, None, :], 0), axis=2)
    start = jnp.sum(jnp.where(own, before[:, None, :], 0), axis=2)
    reach = jnp.where(is_prompt, 0, reach)
    start = jnp.where(is_prompt, 0, start)
    tile_count = rows // tq
    most = jnp.max(reach.reshape(micro, tile_count, tq), axis=2)
    least = jnp.min(start.reshape(micro, tile_count, tq), axis=2)
    end = (jnp.arange(tile_count, dtype=jnp.int32) + 1) * tq
    tiles = jnp.stack(
        [
            (most + tk - 1) // tk,
            least // tk,
            jnp.broadcast_to((end + tk - 1) // tk, (micro, tile_count)),
        ],
        axis=2,
    )
    return jnp.stack([reach, start], axis=1), tiles


GELU_C = 0.7978845608028654
GELU_A = 0.044715


def spread(column, values):
    return jnp.concatenate([wide(column)] * (values.shape[1] // LANES), axis=1)


def lanes_of(values):
    total = values[:, :LANES]
    for c in range(1, values.shape[1] // LANES):
        total = total + values[:, c * LANES : (c + 1) * LANES]
    return total


def norm_tall(z):
    count = z.shape[0]
    mean = jnp.sum(tall_sum(z), axis=0, keepdims=True) / count
    centred = z - mean
    inv = lax.rsqrt(jnp.sum(tall_sum(centred * centred), axis=0, keepdims=True) / count + EPS)
    return centred * inv, inv


def norm_tall_backward(scaled, normed, inv):
    count = scaled.shape[0]
    mean = jnp.sum(tall_sum(scaled), axis=0, keepdims=True) / count
    slope = jnp.sum(tall_sum(scaled * normed), axis=0, keepdims=True) / count
    return inv * (scaled - mean - normed * slope)


def middle_kernel(
    x_ref,
    cot_ref,
    ot_ref,
    mem_ref,
    far_mem_ref,
    win_ref,
    wout_ref,
    wo0_ref,
    wq1_ref,
    wo1_ref,
    wk1_ref,
    wv1_ref,
    small_ref,
    out_ref,
    dso_ref,
    delta_ref,
    skip_ref,
    own_dmk_ref,
    own_dmv_ref,
    far_dmk_ref,
    far_dmv_ref,
    ga_ref,
    gb_ref,
    mk_ref,
    mv_ref,
    mkt_ref,
    mvt_ref,
    wint_ref,
    woutt_ref,
    wo0t_ref,
    wq1t_ref,
    wo1t_ref,
    par_ref,
    fb_ref,
    dmk_ref,
    dmv_ref,
    gpar_ref,
    gfb_ref,
    p_ref,
    act_ref,
    slope_ref,
    mixed_ref,
    dcq_ref,
):
    micro, tile = pl.program_id(0), pl.program_id(1)
    width = x_ref.shape[2]
    hidden = win_ref.shape[1]
    mem_rows = mk_ref.shape[0]
    own_mem = mem_ref.shape[1]
    chunk = width
    half_mem = 256
    size = LANES // 2
    par_count = par_ref.shape[0]
    mem_at = width + hidden

    @pl.when((micro == 0) & (tile == 0))
    def _():
        for ref in (ga_ref, gb_ref, gpar_ref, gfb_ref):
            ref[...] = jnp.zeros_like(ref)
        for here, there in ((wo0_ref, wo0t_ref), (wq1_ref, wq1t_ref), (wo1_ref, wo1t_ref)):
            there[...] = jnp.transpose(here[...])
        for c in range(hidden // chunk):
            part = slice(c * chunk, (c + 1) * chunk)
            wint_ref[part, :] = jnp.transpose(win_ref[:, part])
            woutt_ref[:, part] = jnp.transpose(wout_ref[:, part])
            column = small_ref[:, par_count + c : par_count + c + 1]
            fb_ref[part, :] = low(jnp.broadcast_to(wide(column), (chunk, LANES)))
        for n in range(par_count):
            column = small_ref[:, n : n + 1]
            par_ref[n] = low(jnp.broadcast_to(wide(column), (width, LANES)))

    @pl.when(tile == 0)
    def _():
        dmk_ref[...] = jnp.zeros_like(dmk_ref)
        dmv_ref[...] = jnp.zeros_like(dmv_ref)
        for number, ref in enumerate((mem_ref, far_mem_ref)):
            part = slice(number * own_mem, (number + 1) * own_mem)
            for w_ref, m_ref, mt_ref in ((wk1_ref, mk_ref, mkt_ref), (wv1_ref, mv_ref, mvt_ref)):
                got = low(nn(ref[0], w_ref[...]))
                m_ref[part, :] = got
                mt_ref[:, part] = jnp.transpose(got)

    def par(kind, number, like):
        return spread(par_ref[3 * kind + number], like)

    def note(kind, number, values):
        gpar_ref[3 * kind + number] += lanes_of(values)

    x = wide(jnp.transpose(x_ref[0]))
    self_out = ot_ref[0]
    self_low = low(self_out)
    z = x * par(1, 0, x) + (nn(wo0t_ref[...], self_low) + par(0, 0, x))
    n1, inv1 = norm_tall(z)
    h1 = low(n1 * par(2, 0, x) + par(3, 0, x))
    cq = low(nn(wq1t_ref[...], h1)) * jnp.bfloat16(0.125)
    tops, shares = [], []
    for head in range(HEADS):
        pair = slice(head // 2 * LANES, (head // 2 + 1) * LANES)
        query = alone(cq[pair, :], head % 2)
        top = None
        for c in range(mem_rows // half_mem):
            keys = slice(c * half_mem, (c + 1) * half_mem)
            s = nn(mk_ref[keys, pair], query)
            p_ref[head, keys, :] = s
            here = tall_max(s)
            top = here if top is None else jnp.maximum(top, here)
        tops.append(jnp.max(top, axis=0, keepdims=True))
    for head in range(HEADS):
        part = slice(head * size, (head + 1) * size)
        total, mixed = 0.0, 0.0
        for c in range(mem_rows // half_mem):
            keys = slice(c * half_mem, (c + 1) * half_mem)
            e = jnp.exp(p_ref[head, keys, :] - tops[head])
            p_ref[head, keys, :] = e
            total = total + tall_sum(e)
            mixed = mixed + nn(mvt_ref[part, keys], low(e))
        share = 1.0 / jnp.sum(total, axis=0, keepdims=True)
        shares.append(share)
        mixed_ref[part, :] = mixed * share
    cross = low(mixed_ref[...])
    z = wide(h1) * par(1, 1, x) + (nn(wo1t_ref[...], cross) + par(0, 1, x))
    n2, inv2 = norm_tall(z)
    h2 = low(n2 * par(2, 1, x) + par(3, 1, x))
    branch = 0.0
    for c in range(hidden // chunk):
        part = slice(c * chunk, (c + 1) * chunk)
        pre = nn(wint_ref[part, :], h2)
        pre = pre + spread(fb_ref[part, :], pre)
        square = pre * pre
        gate = 0.5 * jnp.tanh(pre * (square * (GELU_C * GELU_A) + GELU_C)) + 0.5
        act = low(pre * gate)
        act_ref[part, :] = act
        slope_ref[part, :] = gate + (pre * (gate * (1.0 - gate))) * (
            square * (6.0 * GELU_C * GELU_A) + 2.0 * GELU_C
        )
        branch = branch + nn(woutt_ref[:, part], act)
    z = wide(h2) * par(1, 2, x) + (branch + par(0, 2, x))
    n3, inv3 = norm_tall(z)
    out_ref[0] = jnp.transpose(low(n3 * par(2, 2, x) + par(3, 2, x)))

    top = wide(jnp.transpose(cot_ref[0]))
    note(2, 2, top * n3)
    note(3, 2, top)
    dz = norm_tall_backward(top * par(2, 2, x), n3, inv3)
    note(1, 2, dz * wide(h2))
    df = low(dz)
    note(0, 2, wide(df))
    dh = dz * par(1, 2, x)
    for c in range(hidden // chunk):
        part = slice(c * chunk, (c + 1) * chunk)
        dact = low(nn(wout_ref[:, part], df))
        dpre = low(wide(dact) * slope_ref[part, :])
        gfb_ref[part, :] += lanes_of(wide(dpre))
        at = width + c * chunk
        gb_ref[:, at : at + chunk] += nt(act_ref[part, :], df)
        ga_ref[:, part] += nt(h2, dpre)
        dh = dh + nn(win_ref[:, part], dpre)
    note(2, 1, dh * n2)
    note(3, 1, dh)
    dz = norm_tall_backward(dh * par(2, 1, x), n2, inv2)
    note(1, 1, dz * wide(h1))
    dc = low(dz)
    note(0, 1, wide(dc))
    gb_ref[:, :width] += nt(cross, dc)
    dco = low(nn(wo1_ref[...], dc))
    for k in range(HEADS // 2):
        pair = slice(k * LANES, (k + 1) * LANES)
        queries = [alone(cq[pair, :], number) for number in range(2)]
        grads = [alone(dco[pair, :], number) for number in range(2)]
        weighed = wide(dco[pair, :]) * mixed_ref[pair, :]
        dq = [0.0, 0.0]
        for c in range(mem_rows // half_mem):
            keys = slice(c * half_mem, (c + 1) * half_mem)
            for number in range(2):
                head = 2 * k + number
                part = slice(head * size, (head + 1) * size)
                delta = jnp.sum(
                    tall_sum(weighed[number * size : (number + 1) * size]), axis=0, keepdims=True
                )
                p = p_ref[head, keys, :] * shares[head]
                ds = low(p * (nn(mv_ref[keys, pair], grads[number]) - delta))
                dq[number] = dq[number] + nn(mkt_ref[part, keys], ds)
                dmk_ref[keys, pair] += nt(ds, queries[number])
                dmv_ref[keys, pair] += nt(low(p), grads[number])
        for number in range(2):
            head = 2 * k + number
            dcq_ref[head * size : (head + 1) * size, :] = low(dq[number] * 0.125)
    dcq = dcq_ref[...]
    ga_ref[:, hidden + width : hidden + 2 * width] += nt(h1, dcq)
    dh = nn(wq1_ref[...], dcq) + dz * par(1, 1, x)
    note(2, 0, dh * n1)
    note(3, 0, dh)
    dz = norm_tall_backward(dh * par(2, 0, x), n1, inv1)
    note(1, 0, dz * x)
    da = low(dz)
    note(0, 0, wide(da))
    ga_ref[:, hidden : hidden + width] += nt(self_low, da)
    dso = low(nn(wo0_ref[...], da))
    dso_ref[0] = dso
    share = wide(dso) * self_out
    delta_ref[0] = jnp.concatenate(
        [
            jnp.sum(tall_sum(share[h * size : (h + 1) * size]), axis=0, keepdims=True)
            for h in range(HEADS)
        ],
        axis=0,
    )
    skip_ref[0] = jnp.transpose(dz * par(1, 0, x))

    @pl.when(tile == pl.num_programs(1) - 1)
    def _():
        turned = [jnp.transpose(mem_ref[0]), jnp.transpose(far_mem_ref[0])]
        for ref, own, far, at in (
            (dmk_ref, own_dmk_ref, far_dmk_ref, mem_at),
            (dmv_ref, own_dmv_ref, far_dmv_ref, mem_at + width),
        ):
            own_low, far_low = low(ref[:own_mem, :]), low(ref[own_mem:, :])
            own[0] = ref[:own_mem, :]
            far[0] = far_low
            gb_ref[:, at : at + width] += nn(turned[0], own_low) + nn(turned[1], far_low)

    @pl.when((micro == pl.num_programs(0) - 1) & (tile == pl.num_programs(1) - 1))
    def _():
        lane = lax.broadcasted_iota(jnp.int32, (width, LANES), 1)
        small = jnp.zeros((width, LANES), jnp.float32)
        for n in range(par_count):
            small = jnp.where(lane == n, jnp.sum(gpar_ref[n], axis=1, keepdims=True), small)
        for c in range(hidden // chunk):
            column = jnp.sum(gfb_ref[c * chunk : (c + 1) * chunk, :], axis=1, keepdims=True)
            small = jnp.where(lane == par_count + c, column, small)
        gb_ref[:, mem_at + 2 * width :] = small


def middle(x, cot, self_out, memory, far_memory, rest, hidden, block=256):
    micro, rows, width = x.shape
    own_mem = memory.shape[1]
    mem_rows = 2 * own_mem
    f32, bf16 = jnp.float32, jnp.bfloat16
    row_block = pl.BlockSpec((1, block, width), lambda m, i: (m, i, 0))
    tall_block = pl.BlockSpec((1, width, block), lambda m, i: (m, 0, i))
    mem_block = pl.BlockSpec((1, own_mem, width), lambda m, i: (m, 0, 0))

    def fixed(columns, place):
        return pl.BlockSpec(
            (width, columns), lambda m, i: (0, place), pipeline_mode=pl.Buffered(1)
        )

    base = 2 * hidden // width
    columns = [hidden + 2 * width, 3 * width + hidden + LANES]
    mem_out = lambda kind: jax.ShapeDtypeStruct((micro, own_mem, width), kind)
    return pl.pallas_call(
        middle_kernel,
        out_shape=[
            jax.ShapeDtypeStruct((micro, rows, width), bf16),
            jax.ShapeDtypeStruct((micro, width, rows), bf16),
            jax.ShapeDtypeStruct((micro, HEADS, rows), f32),
            jax.ShapeDtypeStruct((micro, rows, width), f32),
            mem_out(f32),
            mem_out(f32),
            mem_out(bf16),
            mem_out(bf16),
        ]
        + [jax.ShapeDtypeStruct((width, n), f32) for n in columns],
        grid=(micro, rows // block),
        in_specs=[row_block, row_block, tall_block, mem_block, mem_block]
        + [fixed(hidden, 0), fixed(hidden, 1)]
        + [fixed(width, base + n) for n in range(5)]
        + [fixed(LANES, (base + 5) * width // LANES)],
        out_specs=[
            row_block,
            tall_block,
            pl.BlockSpec((1, HEADS, block), lambda m, i: (m, 0, i)),
            row_block,
        ]
        + [mem_block] * 4
        + [fixed(n, 0) for n in columns],
        scratch_shapes=[
            pltpu.VMEM((mem_rows, width), bf16),
            pltpu.VMEM((mem_rows, width), bf16),
            pltpu.VMEM((width, mem_rows), bf16),
            pltpu.VMEM((width, mem_rows), bf16),
            pltpu.VMEM((hidden, width), bf16),
            pltpu.VMEM((width, hidden), bf16),
            pltpu.VMEM((width, width), bf16),
            pltpu.VMEM((width, width), bf16),
            pltpu.VMEM((width, width), bf16),
            pltpu.VMEM((12, width, LANES), bf16),
            pltpu.VMEM((hidden, LANES), bf16),
            pltpu.VMEM((mem_rows, width), f32),
            pltpu.VMEM((mem_rows, width), f32),
            pltpu.VMEM((12, width, LANES), f32),
            pltpu.VMEM((hidden, LANES), f32),
            pltpu.VMEM((HEADS, mem_rows, block), f32),
            pltpu.VMEM((hidden, block), bf16),
            pltpu.VMEM((hidden, block), f32),
            pltpu.VMEM((width, block), f32),
            pltpu.VMEM((width, block), bf16),
        ],
        compiler_params=pltpu.CompilerParams(vmem_limit_bytes=60 << 20),
        cost_estimate=pl.CostEstimate(
            flops=6 * micro * rows * width * (3 * width + 2 * hidden + 4 * mem_rows),
            bytes_accessed=20 * micro * rows * width + 30 * width * (width + hidden),
            transcendentals=micro * rows * (HEADS * mem_rows + hidden),
        ),
        name="middle",
    )(x, cot, self_out, memory, far_memory, *[rest] * 8)


def input_grad_kernel(
    dqt_ref, dk_ref, dv_ref, far_dk_ref, far_dv_ref, w_ref, skip_ref, *rest
):
    out_ref = rest[-1]
    width = dk_ref.shape[2]
    dk = low(wide(dk_ref[0]) + wide(far_dk_ref[0]))
    dv = low(wide(dv_ref[0]) + wide(far_dv_ref[0]))
    out_ref[0] = low(
        nt(jnp.transpose(dqt_ref[0]), w_ref[:, :width])
        + nt(dk, w_ref[:, width : 2 * width])
        + nt(dv, w_ref[:, 2 * width :])
        + skip_ref[0]
    )


def input_gradient(number, dqt, dk, dv, far_dk, far_dv, w, skip, so_far, block=512):
    micro, rows, width = skip.shape
    row_block = pl.BlockSpec((1, block, width), lambda i: (0, i, 0))
    place = pl.BlockSpec((1, block, width), lambda i: (number, i, 0))
    before = [] if so_far is None else [so_far]
    return pl.pallas_call(
        input_grad_kernel,
        out_shape=jax.ShapeDtypeStruct((micro, rows, width), jnp.bfloat16),
        grid=(rows // block,),
        in_specs=[pl.BlockSpec((1, width, block), lambda i: (0, 0, i))]
        + [row_block] * 4
        + [
            pl.BlockSpec(w.shape, lambda i: (0, 0), pipeline_mode=pl.Buffered(1)),
            place,
        ]
        + [pl.BlockSpec(memory_space=pl.ANY)] * len(before),
        out_specs=place,
        input_output_aliases={7: 0} if before else {},
        compiler_params=pltpu.CompilerParams(vmem_limit_bytes=VMEM_LIMIT),
        cost_estimate=pl.CostEstimate(
            flops=6 * rows * width * width,
            bytes_accessed=16 * rows * width + 6 * width * width,
            transcendentals=0,
        ),
        name="input_gradient",
    )(dqt, dk, dv, far_dk, far_dv, w, skip, *before)


def total_tn(left, right):
    return tn(left.reshape(-1, left.shape[-1]), right.reshape(-1, right.shape[-1]))


def flat_nn(left, right):
    return nn(left.reshape(-1, left.shape[-1]), right).reshape(left.shape[:-1] + (right.shape[1],))


def flat_nt(left, right):
    return nt(left.reshape(-1, left.shape[-1]), right).reshape(left.shape[:-1] + (right.shape[0],))


def body(
    layer_in,
    memory,
    seg_ids,
    offsets,
    cotangent,
    attn_q,
    attn_k,
    attn_v,
    attn_o,
    w_in,
    w_out,
    ffn_bias,
    out_bias,
    omega,
    ln_gain,
    ln_bias,
):
    axis = "dp"
    is_prompt = lax.axis_index(axis) % 2 == 1
    own_rows = attn_q.shape[1]
    width = attn_q.shape[2]
    hidden = w_in.shape[1]
    mem_rows = memory.shape[1]

    packed = jnp.concatenate([attn_q[0], attn_k[0], attn_v[0]], axis=1)
    packed, w_in, w_out, small_parts, layer_in, memory = lax.optimization_barrier(
        (packed, w_in, w_out, (out_bias, omega, ln_gain, ln_bias, ffn_bias), layer_in, memory)
    )
    first = tree_gather(packed, axis)
    far_x = prompt_to_continuation(layer_in, axis)
    far_memory = from_partner(memory, axis, 0)
    parts = hidden // width
    small = jnp.concatenate(
        [p.T for p in small_parts[:4]] + [small_parts[4].reshape(own_rows, -1)], axis=1
    )
    small_cols = small.shape[1]
    rest = lax.all_gather(
        jnp.concatenate(
            [
                jnp.swapaxes(w_in.reshape(own_rows, width, parts), 1, 2).reshape(own_rows, -1),
                w_out.reshape(own_rows, -1),
                attn_o[0],
                attn_q[1],
                attn_o[1],
                attn_k[1],
                attn_v[1],
                jnp.pad(small, ((0, 0), (0, LANES - small_cols))),
            ],
            axis=1,
        ),
        axis,
        axis=0,
        tiled=True,
    )
    limits, tiles = mask_limits(seg_ids[:, 0], offsets[:, 0], is_prompt)
    qt, kv, kvt, far_kv, far_kvt = project(layer_in, far_x, first)
    self_out, lse = self_forward(qt, kv, kvt, far_kv, far_kvt, limits, tiles)
    (
        final,
        dso,
        delta,
        skip,
        own_mk,
        own_mv,
        far_mk,
        far_mv,
        g_a,
        g_b,
    ) = middle(layer_in, cotangent, self_out, memory, far_memory, rest, hidden)

    ready = TreeScatter([g_a, g_b], [0, 1], axis)
    back, far = [], []
    for number in range(layer_in.shape[0]):
        dso, _ = ready.send(dso)
        back.append(
            self_backward(
                number,
                qt,
                kv,
                kvt,
                far_kv,
                far_kvt,
                dso,
                lse,
                delta,
                limits,
                tiles,
                layer_in,
                far_x,
            )
        )
        ready.receive(back[number][0])
        far.append(continuation_to_prompt(back[number][1:3], axis))
    mem_dk = low(own_mk + wide(from_partner(far_mk, axis, 0)))
    mem_dv = low(own_mv + wide(from_partner(far_mv, axis, 0)))
    at = 2 * hidden + 3 * width
    memory_grad = low(
        flat_nt(mem_dk, rest[:, at : at + width])
        + flat_nt(mem_dv, rest[:, at + width : at + 2 * width])
    )
    late = TreeScatter([sum(b[5] for b in back)], [0], axis)
    input_grad = None
    for number, (b, f) in enumerate(zip(back, far)):
        input_grad = input_gradient(
            number, b[0], b[3], b[4], f[0], f[1], first, skip, input_grad
        )
    s_a, s_b = ready.finish()
    (s_c,) = late.finish()
    s_q0, s_k0, s_v0 = (s_c[:, k * width : (k + 1) * width] for k in range(3))
    s_in = jnp.swapaxes(s_a[:, :hidden].reshape(own_rows, parts, width), 1, 2)
    s_in = s_in.reshape(own_rows, hidden)
    s_o0, s_q1 = s_a[:, hidden : hidden + width], s_a[:, hidden + width :]
    s_o1 = s_b[:, :width]
    s_out = s_b[:, width : width + hidden].reshape(w_out.shape)
    s_k1, s_v1 = (s_b[:, hidden + k * width :][:, :width] for k in (1, 2))
    s_small = s_b[:, hidden + 3 * width :][:, :small_cols]
    return (
        final,
        input_grad,
        memory_grad,
        jnp.stack([s_q0, s_q1]),
        jnp.stack([s_k0, s_k1]),
        jnp.stack([s_v0, s_v1]),
        jnp.stack([s_o0, s_o1]),
        s_in,
        s_out,
        s_small[:, 12:].reshape(-1),
        s_small[:, 0:3].T,
        s_small[:, 3:6].T,
        s_small[:, 6:9].T,
        s_small[:, 9:12].T,
    )


def solution(mesh):
    rows = P(None, "dp", None)
    small = P(None, "dp")
    return jax.shard_map(
        body,
        mesh=mesh,
        in_specs=(rows,) * 9 + (P("dp", None), P("dp", None), P("dp"), small, small, small, small),
        out_specs=(rows,) * 7 + (P("dp", None), P("dp", None), P("dp"), small, small, small, small),
        check_vma=False,
    )
```

```python
import functools

import jax
import jax.numpy as jnp
from jax import lax
from jax.experimental import pallas as pl
from jax.experimental.pallas import tpu as pltpu
from jax.sharding import PartitionSpec as P

HEADS = 8
EPS = 1e-05
NEG = -1e30
LANES = 128
VMEM_LIMIT = 56 << 20


def nn(left, right):
    return lax.dot_general(
        left, right, (((1,), (0,)), ((), ())), preferred_element_type=jnp.float32
    )


def nt(left, right):
    return lax.dot_general(
        left, right, (((1,), (1,)), ((), ())), preferred_element_type=jnp.float32
    )


def tn(left, right):
    return lax.dot_general(
        left, right, (((0,), (0,)), ((), ())), preferred_element_type=jnp.float32
    )


def low(values):
    return values.astype(jnp.bfloat16)


def wide(values):
    return values.astype(jnp.float32)


def stages_of(axis):
    bits = (lax.axis_size(axis) - 1).bit_length()
    return [(0, 1)] + [(bit, min(2, bits - bit)) for bit in range(1, bits, 2)]


def from_partner(x, axis, bit):
    return lax.ppermute(x, axis, [(i, i ^ 1 << bit) for i in range(lax.axis_size(axis))])


def prompt_to_continuation(x, axis):
    return lax.ppermute(x, axis, [(i + 1, i) for i in range(0, lax.axis_size(axis), 2)])


def continuation_to_prompt(x, axis):
    return lax.ppermute(x, axis, [(i, i + 1) for i in range(0, lax.axis_size(axis), 2)])


def shifted(x, axis, offset):
    return lax.ppermute(x, axis, [(i, i ^ offset) for i in range(lax.axis_size(axis))])


def tree_gather(x, axis):
    stages = stages_of(axis)
    me = lax.axis_index(axis)
    block = x.reshape((1,) * len(stages) + x.shape)
    for number in reversed(range(len(stages))):
        bit, count = stages[number]
        dim = len(stages) - 1 - number
        place = (me >> bit) & ((1 << count) - 1)
        parts = [block] + [shifted(block, axis, k << bit) for k in range(1, 1 << count)]
        out = []
        for spot in range(1 << count):
            piece = parts[spot]
            for mine in range(1, 1 << count):
                piece = jnp.where(place == mine, parts[spot ^ mine], piece)
            out.append(piece)
        block = jnp.concatenate(out, dim)
    return block.reshape((-1,) + x.shape[1:])


class TreeScatter:
    def __init__(self, array, axis):
        self.axis = axis
        self.stages = stages_of(axis)
        self.me = lax.axis_index(axis)
        self.own = (array.shape[0] // lax.axis_size(axis),) + array.shape[1:]
        sizes = tuple(1 << count for _, count in reversed(self.stages))
        self.block = array.reshape(sizes + self.own)
        self.number = 0

    def send(self, after=None):
        bit, count = self.stages[self.number]
        dim = len(self.stages) - 1 - self.number
        place = (self.me >> bit) & ((1 << count) - 1)
        pick = lambda k: lax.dynamic_index_in_dim(self.block, place ^ k, dim, keepdims=True)
        aways = [low(pick(k)) for k in range(1, 1 << count)]
        if after is not None:
            after, aways = lax.optimization_barrier((after, aways))
        self.keep = pick(0)
        self.got = [shifted(a, self.axis, k << bit) for k, a in enumerate(aways, 1)]
        return after

    def receive(self, behind=None):
        if behind is not None:
            self.got, _ = lax.optimization_barrier((self.got, behind))
        self.block = sum([wide(g) for g in self.got], self.keep)
        self.number += 1

    def finish(self):
        while self.number < len(self.stages):
            self.send()
            self.receive()
        return self.block.reshape(self.own)


def tall_sum(values):
    return jnp.sum(values.reshape(-1, 8, values.shape[1]), axis=0)


def tall_max(values):
    return jnp.max(values.reshape(-1, 8, values.shape[1]), axis=0)


def alone(pair, number):
    half = pair.shape[0] // 2
    blank = jnp.zeros((half, pair.shape[1]), pair.dtype)
    if number == 0:
        return jnp.concatenate([pair[:half], blank], axis=0)
    return jnp.concatenate([blank, pair[half:]], axis=0)


def project_kernel(x_ref, far_ref, w_ref, qt_ref, kv_ref, kvt_ref, fkv_ref, fkvt_ref):
    width = x_ref.shape[2]
    for c in range(3):
        part = slice(c * width, (c + 1) * width)
        here = low(nn(x_ref[0], w_ref[:, part]))
        if c == 0:
            qt_ref[0] = jnp.transpose(here)
            continue
        into = slice((c - 1) * width, c * width)
        kv_ref[0, :, into] = here
        kvt_ref[0, into, :] = jnp.transpose(here)
        there = low(nn(far_ref[0], w_ref[:, part]))
        fkv_ref[0, :, into] = there
        fkvt_ref[0, into, :] = jnp.transpose(there)


def project(x, far, w, block=512):
    micro, rows, width = x.shape
    tall = lambda n: jax.ShapeDtypeStruct((micro, n, rows), jnp.bfloat16)
    long = jax.ShapeDtypeStruct((micro, rows, 2 * width), jnp.bfloat16)
    rows_in = pl.BlockSpec((1, block, width), lambda m, i: (m, i, 0))
    rows_out = pl.BlockSpec((1, block, 2 * width), lambda m, i: (m, i, 0))
    turned = lambda n: pl.BlockSpec((1, n, block), lambda m, i: (m, 0, i))
    return pl.pallas_call(
        project_kernel,
        out_shape=(tall(width), long, tall(2 * width), long, tall(2 * width)),
        grid=(micro, rows // block),
        in_specs=[
            rows_in,
            rows_in,
            pl.BlockSpec(w.shape, lambda m, i: (0, 0), pipeline_mode=pl.Buffered(1)),
        ],
        out_specs=[turned(width), rows_out, turned(2 * width), rows_out, turned(2 * width)],
        compiler_params=pltpu.CompilerParams(vmem_limit_bytes=VMEM_LIMIT),
        cost_estimate=pl.CostEstimate(
            flops=2 * 5 * micro * rows * width * width,
            bytes_accessed=22 * micro * rows * width,
            transcendentals=0,
        ),
        name="project",
    )(x, far, w)


def self_forward_kernel(
    tq, tk, pairs, tiles, qt_ref, kp_ref, kl_ref, vtp_ref, vtl_ref, lim_ref, ot_ref, lse_ref, s_ref, e_ref
):
    micro, tile = pl.program_id(0), pl.program_id(1)
    prefix_rows = kp_ref.shape[1]
    prefix_tiles = tiles[micro, tile, 0]
    local_first, local_end = tiles[micro, tile, 1], tiles[micro, tile, 2]
    reach, start = lim_ref[0, 0:1, :], lim_ref[0, 1:2, :]
    rows = tile * tq + lax.broadcasted_iota(jnp.int32, (1, tq), 1)
    key_at = lax.broadcasted_iota(jnp.int32, (tk, tq), 0)
    heads = 2 * pairs
    size = LANES // 2

    def prefix_mask(j):
        return key_at < reach - j * tk

    def local_mask(j):
        return (key_at <= rows - j * tk) & (key_at >= start - j * tk)

    ot_ref[0] = jnp.zeros((ot_ref.shape[1], tq), jnp.float32)
    for group in range(HEADS // heads):
        queries = []
        for h in range(heads):
            p = group * pairs + h // 2
            pair = qt_ref[0, p * LANES : (p + 1) * LANES, :] * jnp.bfloat16(0.125)
            queries.append(alone(pair, h % 2))

        def score(k_ref, offset, masker, j, tops):
            base = pl.multiple_of(j * tk, tk)
            seen = masker(j)
            out = []
            for h in range(heads):
                p = group * pairs + h // 2
                s = nn(k_ref[0, pl.ds(base, tk), p * LANES : (p + 1) * LANES], queries[h])
                s = jnp.where(seen, s, NEG)
                s_ref[h, pl.ds(pl.multiple_of(offset + base, tk), tk), :] = s
                out.append(jnp.maximum(tops[h], tall_max(s)))
            return tuple(out)

        tops = tuple(jnp.full((8, tq), NEG, jnp.float32) for _ in range(heads))
        tops = lax.fori_loop(
            0, prefix_tiles, functools.partial(score, kp_ref, 0, prefix_mask), tops
        )
        tops = lax.fori_loop(
            local_first,
            local_end,
            functools.partial(score, kl_ref, prefix_rows, local_mask),
            tops,
        )
        tops = [jnp.max(t, axis=0, keepdims=True) for t in tops]

        def mix(vt_ref, offset, j, carry):
            base = pl.multiple_of(j * tk, tk)
            out = []
            for h in range(heads):
                e = jnp.exp(
                    s_ref[h, pl.ds(pl.multiple_of(offset + base, tk), tk), :] - tops[h]
                )
                out.append(carry[h] + tall_sum(e))
                e_ref[h] = low(e)
            for h in range(heads):
                head = group * heads + h
                part = slice(head * size, (head + 1) * size)
                ot_ref[0, part, :] += nn(vt_ref[0, part, pl.ds(base, tk)], e_ref[h])
            return tuple(out)

        carry = (jnp.zeros((8, tq), jnp.float32),) * heads
        carry = lax.fori_loop(0, prefix_tiles, functools.partial(mix, vtp_ref, 0), carry)
        carry = lax.fori_loop(
            local_first, local_end, functools.partial(mix, vtl_ref, prefix_rows), carry
        )
        for h in range(heads):
            head = group * heads + h
            total = jnp.sum(carry[h], axis=0, keepdims=True)
            part = slice(head * size, (head + 1) * size)
            ot_ref[0, part, :] = ot_ref[0, part, :] / total
            lse_ref[0, head : head + 1, :] = tops[h] + jnp.log(total)


def self_forward(qt, kv, kvt, far_kv, far_kvt, limits, tiles, tq=256, tk=256, pairs=4):
    micro, width, rows = qt.shape
    return pl.pallas_call(
        functools.partial(self_forward_kernel, tq, tk, pairs),
        out_shape=(
            jax.ShapeDtypeStruct((micro, width, rows), jnp.float32),
            jax.ShapeDtypeStruct((micro, HEADS, rows), jnp.float32),
        ),
        grid_spec=pltpu.PrefetchScalarGridSpec(
            num_scalar_prefetch=1,
            grid=(micro, rows // tq),
            in_specs=[
                pl.BlockSpec((1, width, tq), lambda m, i, s: (m, 0, i)),
                pl.BlockSpec((1, rows, width), lambda m, i, s: (m, 0, 0)),
                pl.BlockSpec((1, rows, width), lambda m, i, s: (m, 0, 0)),
                pl.BlockSpec((1, width, rows), lambda m, i, s: (m, 1, 0)),
                pl.BlockSpec((1, width, rows), lambda m, i, s: (m, 1, 0)),
                pl.BlockSpec((1, 2, tq), lambda m, i, s: (m, 0, i)),
            ],
            out_specs=[
                pl.BlockSpec((1, width, tq), lambda m, i, s: (m, 0, i)),
                pl.BlockSpec((1, HEADS, tq), lambda m, i, s: (m, 0, i)),
            ],
            scratch_shapes=[
                pltpu.VMEM((2 * pairs, 2 * rows, tq), jnp.float32),
                pltpu.VMEM((2 * pairs, tk, tq), jnp.bfloat16),
            ],
        ),
        compiler_params=pltpu.CompilerParams(vmem_limit_bytes=VMEM_LIMIT),
        cost_estimate=pl.CostEstimate(
            flops=4 * micro * rows * rows * width,
            bytes_accessed=16 * micro * rows * width,
            transcendentals=micro * rows * rows * HEADS,
        ),
        name="self_forward",
    )(tiles, qt, far_kv, kv, far_kvt, kvt, limits)


def self_backward_kernel(
    tq,
    tk,
    pairs,
    tiles,
    qt_ref,
    kp_ref,
    vp_ref,
    kl_ref,
    vl_ref,
    ktp_ref,
    ktl_ref,
    dot_ref,
    lse_ref,
    delta_ref,
    lim_ref,
    x_ref,
    far_ref,
    dqt_ref,
    dkp_ref,
    dvp_ref,
    dkl_ref,
    dvl_ref,
    g_ref,
    sum_kp,
    sum_vp,
    sum_kl,
    sum_vl,
    sum_q,
    s_ref,
    dp_ref,
    p_ref,
    ds_ref,
):
    micro = pl.program_id(0)
    row_count = qt_ref.shape[2]
    size = LANES // 2

    @pl.when(micro == 0)
    def _():
        g_ref[...] = jnp.zeros_like(g_ref)

    for ref in (sum_kp, sum_vp, sum_kl, sum_vl):
        ref[...] = jnp.zeros_like(ref)
    key_at = lax.broadcasted_iota(jnp.int32, (tk, tq), 0)
    for i in range(row_count // tq):
        here = slice(i * tq, (i + 1) * tq)
        prefix_tiles = tiles[micro, i, 0]
        local_first, local_end = tiles[micro, i, 1], tiles[micro, i, 2]
        reach, start = lim_ref[0, 0:1, here], lim_ref[0, 1:2, here]
        rows = i * tq + lax.broadcasted_iota(jnp.int32, (1, tq), 1)
        queries, grads, totals, deltas = [], [], [], []
        for h in range(2 * pairs):
            part = slice(h // 2 * LANES, (h // 2 + 1) * LANES)
            queries.append(alone(qt_ref[0, part, here] * jnp.bfloat16(0.125), h % 2))
            grads.append(alone(dot_ref[0, part, here], h % 2))
            totals.append(lse_ref[0, 0, h : h + 1, here])
            deltas.append(delta_ref[0, 0, h : h + 1, here])
        sum_q[...] = jnp.zeros_like(sum_q)

        def body(k_ref, v_ref, kt_ref, sum_k, sum_v, masker, j, _):
            base = pl.multiple_of(j * tk, tk)
            seen = masker(j)
            heads = 2 * pairs
            cols = [slice(h // 2 * LANES, (h // 2 + 1) * LANES) for h in range(heads)]
            for h in range(heads):
                s_ref[h] = nn(k_ref[0, pl.ds(base, tk), cols[h]], queries[h])
                dp_ref[h] = nn(v_ref[0, pl.ds(base, tk), cols[h]], grads[h])
            for h in range(heads):
                p = jnp.exp(jnp.where(seen, s_ref[h], NEG) - totals[h])
                p_ref[h] = low(p)
                ds_ref[h] = low(p * (dp_ref[h] - deltas[h]))
            for h in range(heads):
                part = slice(h * size, (h + 1) * size)
                sum_v[pl.ds(base, tk), cols[h]] += nt(p_ref[h], grads[h])
                sum_k[pl.ds(base, tk), cols[h]] += nt(ds_ref[h], queries[h])
                sum_q[part, :] += nn(kt_ref[0, part, pl.ds(base, tk)], ds_ref[h])
            return 0

        def prefix_mask(j):
            return key_at < reach - j * tk

        def local_mask(j):
            return (key_at <= rows - j * tk) & (key_at >= start - j * tk)

        lax.fori_loop(
            0,
            prefix_tiles,
            functools.partial(body, kp_ref, vp_ref, ktp_ref, sum_kp, sum_vp, prefix_mask),
            0,
        )
        lax.fori_loop(
            local_first,
            local_end,
            functools.partial(body, kl_ref, vl_ref, ktl_ref, sum_kl, sum_vl, local_mask),
            0,
        )
        dqt_ref[0, :, here] = low(sum_q[...] * 0.125)
    dkp_ref[0] = low(sum_kp[...])
    dvp_ref[0] = low(sum_vp[...])
    dkl_ref[0] = low(sum_kl[...])
    dvl_ref[0] = low(sum_vl[...])
    width = x_ref.shape[2]
    own, far = jnp.transpose(x_ref[0]), jnp.transpose(far_ref[0])
    g_ref[:, :width] += nt(own, dqt_ref[0])
    g_ref[:, width : 2 * width] += nn(own, dkl_ref[0]) + nn(far, dkp_ref[0])
    g_ref[:, 2 * width :] += nn(own, dvl_ref[0]) + nn(far, dvp_ref[0])


def self_backward(qt, kv, kvt, far_kv, far_kvt, grad_out, lse, delta, limits, tiles, x, far_x):
    tq, tk, pairs = 256, 256, HEADS // 2
    micro, width, rows = qt.shape
    tall = pl.BlockSpec((1, width, rows), lambda m, s: (m, 0, 0))
    long = lambda place: pl.BlockSpec((1, rows, width), lambda m, s: (m, 0, place))
    line = pl.BlockSpec((1, 1, HEADS, rows), lambda m, s: (m, 0, 0, 0))
    bf16 = jax.ShapeDtypeStruct((micro, rows, width), jnp.bfloat16)
    return pl.pallas_call(
        functools.partial(self_backward_kernel, tq, tk, pairs),
        out_shape=(
            jax.ShapeDtypeStruct((micro, width, rows), jnp.bfloat16),
            bf16,
            bf16,
            bf16,
            bf16,
            jax.ShapeDtypeStruct((width, 3 * width), jnp.float32),
        ),
        grid_spec=pltpu.PrefetchScalarGridSpec(
            num_scalar_prefetch=1,
            grid=(micro,),
            in_specs=[
                tall,
                long(0),
                long(1),
                long(0),
                long(1),
                tall,
                tall,
                tall,
                line,
                line,
                pl.BlockSpec((1, 2, rows), lambda m, s: (m, 0, 0)),
                long(0),
                long(0),
            ],
            out_specs=[tall]
            + [long(0)] * 4
            + [
                pl.BlockSpec(
                    (width, 3 * width), lambda m, s: (0, 0), pipeline_mode=pl.Buffered(1)
                )
            ],
            scratch_shapes=[pltpu.VMEM((rows, width), jnp.float32)] * 4
            + [pltpu.VMEM((width, tq), jnp.float32)]
            + [pltpu.VMEM((HEADS, tk, tq), t) for t in (jnp.float32, jnp.float32)]
            + [pltpu.VMEM((HEADS, tk, tq), t) for t in (jnp.bfloat16, jnp.bfloat16)],
        ),
        compiler_params=pltpu.CompilerParams(vmem_limit_bytes=60 << 20),
        cost_estimate=pl.CostEstimate(
            flops=10 * micro * rows * rows * width,
            bytes_accessed=40 * micro * rows * width,
            transcendentals=micro * rows * rows * HEADS,
        ),
        name="self_backward",
    )(
        tiles,
        qt,
        far_kv,
        far_kv,
        kv,
        kv,
        far_kvt,
        kvt,
        grad_out,
        lse[:, None],
        delta[:, None],
        limits,
        x,
        far_x,
    )


def mask_limits(seg, off, is_prompt, tq=256, tk=256):
    micro, rows = seg.shape
    index = jnp.arange(off.shape[1], dtype=jnp.int32)
    own = seg[:, :, None] == index
    count = jnp.sum(own.astype(jnp.int32), axis=1)
    before = jnp.sum(jnp.where(index[:, None] > index[None, :], count[:, None, :], 0), axis=2)
    reach = jnp.sum(jnp.where(own, off[:, None, :], 0), axis=2)
    start = jnp.sum(jnp.where(own, before[:, None, :], 0), axis=2)
    reach = jnp.where(is_prompt, 0, reach)
    start = jnp.where(is_prompt, 0, start)
    tile_count = rows // tq
    most = jnp.max(reach.reshape(micro, tile_count, tq), axis=2)
    least = jnp.min(start.reshape(micro, tile_count, tq), axis=2)
    end = (jnp.arange(tile_count, dtype=jnp.int32) + 1) * tq
    tiles = jnp.stack(
        [
            (most + tk - 1) // tk,
            least // tk,
            jnp.broadcast_to((end + tk - 1) // tk, (micro, tile_count)),
        ],
        axis=2,
    )
    return jnp.stack([reach, start], axis=1), tiles


GELU_C = 0.7978845608028654
GELU_A = 0.044715


def spread(column, values):
    return jnp.concatenate([wide(column)] * (values.shape[1] // LANES), axis=1)


def lanes_of(values):
    total = values[:, :LANES]
    for c in range(1, values.shape[1] // LANES):
        total = total + values[:, c * LANES : (c + 1) * LANES]
    return total


def norm_tall(z):
    count = z.shape[0]
    mean = jnp.sum(tall_sum(z), axis=0, keepdims=True) / count
    centred = z - mean
    inv = lax.rsqrt(jnp.sum(tall_sum(centred * centred), axis=0, keepdims=True) / count + EPS)
    return centred * inv, inv


def norm_tall_backward(scaled, normed, inv):
    count = scaled.shape[0]
    mean = jnp.sum(tall_sum(scaled), axis=0, keepdims=True) / count
    slope = jnp.sum(tall_sum(scaled * normed), axis=0, keepdims=True) / count
    return inv * (scaled - mean - normed * slope)


def middle_kernel(
    x_ref,
    cot_ref,
    ot_ref,
    mem_ref,
    far_mem_ref,
    win_ref,
    wout_ref,
    wo0_ref,
    wq1_ref,
    wo1_ref,
    wk1_ref,
    wv1_ref,
    small_ref,
    out_ref,
    dso_ref,
    delta_ref,
    skip_ref,
    own_dmk_ref,
    own_dmv_ref,
    far_dmk_ref,
    far_dmv_ref,
    g_out_ref,
    mk_ref,
    mv_ref,
    mkt_ref,
    mvt_ref,
    wint_ref,
    woutt_ref,
    wo0t_ref,
    wq1t_ref,
    wo1t_ref,
    par_ref,
    fb_ref,
    dmk_ref,
    dmv_ref,
    gpar_ref,
    gfb_ref,
    p_ref,
    act_ref,
    slope_ref,
    mixed_ref,
    work_ref,
    g_ref,
    sems,
):
    micro, tile = pl.program_id(0), pl.program_id(1)
    width = x_ref.shape[2]
    hidden = win_ref.shape[1]
    mem_rows = mk_ref.shape[0]
    own_mem = mem_ref.shape[1]
    chunk = width
    half_mem = 256
    size = LANES // 2
    par_count = par_ref.shape[0]
    block = x_ref.shape[1]
    base = 2 * hidden
    mem_at = base + 3 * width

    @pl.when((micro == 0) & (tile == 0))
    def _():
        for ref in (g_ref, gpar_ref, gfb_ref):
            ref[...] = jnp.zeros_like(ref)
        for here, there in ((wo0_ref, wo0t_ref), (wq1_ref, wq1t_ref), (wo1_ref, wo1t_ref)):
            there[...] = jnp.transpose(here[...])
        for c in range(hidden // chunk):
            part = slice(c * chunk, (c + 1) * chunk)
            wint_ref[part, :] = jnp.transpose(win_ref[:, part])
            woutt_ref[:, part] = jnp.transpose(wout_ref[:, part])
            column = small_ref[:, par_count + c : par_count + c + 1]
            fb_ref[part, :] = low(jnp.broadcast_to(wide(column), (chunk, LANES)))
        for n in range(par_count):
            column = small_ref[:, n : n + 1]
            par_ref[n] = low(jnp.broadcast_to(wide(column), (width, LANES)))

    @pl.when(tile == 0)
    def _():
        dmk_ref[...] = jnp.zeros_like(dmk_ref)
        dmv_ref[...] = jnp.zeros_like(dmv_ref)
        for number, ref in enumerate((mem_ref, far_mem_ref)):
            part = slice(number * own_mem, (number + 1) * own_mem)
            for w_ref, m_ref, mt_ref in ((wk1_ref, mk_ref, mkt_ref), (wv1_ref, mv_ref, mvt_ref)):
                got = low(nn(ref[0], w_ref[...]))
                m_ref[part, :] = got
                mt_ref[:, part] = jnp.transpose(got)

    def par(kind, number, like):
        return spread(par_ref[3 * kind + number], like)

    def note(kind, number, values):
        gpar_ref[3 * kind + number] += lanes_of(values)

    x = wide(jnp.transpose(x_ref[0]))
    self_out = ot_ref[0]
    self_low = low(self_out)
    z = x * par(1, 0, x) + (nn(wo0t_ref[...], self_low) + par(0, 0, x))
    n1, inv1 = norm_tall(z)
    h1 = low(n1 * par(2, 0, x) + par(3, 0, x))
    cq = low(nn(wq1t_ref[...], h1)) * jnp.bfloat16(0.125)
    tops, shares = [], []
    for head in range(HEADS):
        pair = slice(head // 2 * LANES, (head // 2 + 1) * LANES)
        query = alone(cq[pair, :], head % 2)
        top = None
        for c in range(mem_rows // half_mem):
            keys = slice(c * half_mem, (c + 1) * half_mem)
            s = nn(mk_ref[keys, pair], query)
            p_ref[head, keys, :] = s
            here = tall_max(s)
            top = here if top is None else jnp.maximum(top, here)
        tops.append(jnp.max(top, axis=0, keepdims=True))
    for head in range(HEADS):
        part = slice(head * size, (head + 1) * size)
        total, mixed = 0.0, 0.0
        for c in range(mem_rows // half_mem):
            keys = slice(c * half_mem, (c + 1) * half_mem)
            e = jnp.exp(p_ref[head, keys, :] - tops[head])
            p_ref[head, keys, :] = e
            total = total + tall_sum(e)
            mixed = mixed + nn(mvt_ref[part, keys], low(e))
        share = 1.0 / jnp.sum(total, axis=0, keepdims=True)
        shares.append(share)
        mixed_ref[part, :] = mixed * share
    cross = low(mixed_ref[...])
    z = wide(h1) * par(1, 1, x) + (nn(wo1t_ref[...], cross) + par(0, 1, x))
    n2, inv2 = norm_tall(z)
    h2 = low(n2 * par(2, 1, x) + par(3, 1, x))
    for c in range(hidden // chunk):
        part = slice(c * chunk, (c + 1) * chunk)
        slope_ref[part, :] = nn(wint_ref[part, :], h2)
    for c in range(hidden // chunk):
        part = slice(c * chunk, (c + 1) * chunk)
        pre = slope_ref[part, :]
        pre = pre + spread(fb_ref[part, :], pre)
        square = pre * pre
        gate = 0.5 * jnp.tanh(pre * (square * (GELU_C * GELU_A) + GELU_C)) + 0.5
        act_ref[part, :] = low(pre * gate)
        slope_ref[part, :] = gate + (pre * (gate * (1.0 - gate))) * (
            square * (6.0 * GELU_C * GELU_A) + 2.0 * GELU_C
        )
    branch = nn(woutt_ref[...], act_ref[...])
    z = wide(h2) * par(1, 2, x) + (branch + par(0, 2, x))
    n3, inv3 = norm_tall(z)
    out_ref[0] = jnp.transpose(low(n3 * par(2, 2, x) + par(3, 2, x)))

    top = wide(jnp.transpose(cot_ref[0]))
    note(2, 2, top * n3)
    note(3, 2, top)
    dz = norm_tall_backward(top * par(2, 2, x), n3, inv3)
    note(1, 2, dz * wide(h2))
    df = low(dz)
    note(0, 2, wide(df))
    for c in range(hidden // chunk):
        part = slice(c * chunk, (c + 1) * chunk)
        work_ref[part, :] = low(nn(wout_ref[:, part], df))
    for c in range(hidden // chunk):
        part = slice(c * chunk, (c + 1) * chunk)
        dpre = low(wide(work_ref[part, :]) * slope_ref[part, :])
        gfb_ref[part, :] += lanes_of(wide(dpre))
        work_ref[part, :] = dpre
    dh = dz * par(1, 2, x) + nn(win_ref[...], work_ref[...])
    for c in range(hidden // chunk):
        part = slice(c * chunk, (c + 1) * chunk)
        at = hidden + c * chunk
        g_ref[:, at : at + chunk] += nt(act_ref[part, :], df)
        g_ref[:, part] += nt(h2, work_ref[part, :])
    note(2, 1, dh * n2)
    note(3, 1, dh)
    dz = norm_tall_backward(dh * par(2, 1, x), n2, inv2)
    note(1, 1, dz * wide(h1))
    dc = low(dz)
    note(0, 1, wide(dc))
    g_ref[:, base + 2 * width : base + 3 * width] += nt(cross, dc)
    dco = low(nn(wo1_ref[...], dc))
    queries = [alone(cq[h // 2 * LANES : (h // 2 + 1) * LANES], h % 2) for h in range(HEADS)]
    grads = [alone(dco[h // 2 * LANES : (h // 2 + 1) * LANES], h % 2) for h in range(HEADS)]
    weighed = wide(dco) * mixed_ref[...]
    deltas = [
        jnp.sum(tall_sum(weighed[h * size : (h + 1) * size]), axis=0, keepdims=True)
        for h in range(HEADS)
    ]
    mixed_ref[...] = jnp.zeros_like(mixed_ref)
    for c in range(mem_rows // half_mem):
        keys = slice(c * half_mem, (c + 1) * half_mem)
        spot = [slice(h * half_mem, (h + 1) * half_mem) for h in range(HEADS)]
        cols = [slice(h // 2 * LANES, (h // 2 + 1) * LANES) for h in range(HEADS)]
        for h in range(HEADS):
            slope_ref[spot[h], :] = nn(mv_ref[keys, cols[h]], grads[h])
        for h in range(HEADS):
            p = p_ref[h, keys, :] * shares[h]
            act_ref[spot[h], :] = low(p)
            work_ref[spot[h], :] = low(p * (slope_ref[spot[h], :] - deltas[h]))
        for h in range(HEADS):
            part = slice(h * size, (h + 1) * size)
            dmv_ref[keys, cols[h]] += nt(act_ref[spot[h], :], grads[h])
            dmk_ref[keys, cols[h]] += nt(work_ref[spot[h], :], queries[h])
            mixed_ref[part, :] += nn(mkt_ref[part, keys], work_ref[spot[h], :])
    dcq = low(mixed_ref[...] * 0.125)
    g_ref[:, base + width : base + 2 * width] += nt(h1, dcq)
    dh = nn(wq1_ref[...], dcq) + dz * par(1, 1, x)
    note(2, 0, dh * n1)
    note(3, 0, dh)
    dz = norm_tall_backward(dh * par(2, 0, x), n1, inv1)
    note(1, 0, dz * x)
    da = low(dz)
    note(0, 0, wide(da))
    g_ref[:, base : base + width] += nt(self_low, da)
    dso = low(nn(wo0_ref[...], da))
    dso_ref[0] = dso
    share = wide(dso) * self_out
    delta_ref[0] = jnp.concatenate(
        [
            jnp.sum(tall_sum(share[h * size : (h + 1) * size]), axis=0, keepdims=True)
            for h in range(HEADS)
        ],
        axis=0,
    )
    skip_ref[0] = jnp.transpose(dz * par(1, 0, x))

    @pl.when(tile == pl.num_programs(1) - 1)
    def _():
        turned = [jnp.transpose(mem_ref[0]), jnp.transpose(far_mem_ref[0])]
        for ref, own, far, at in (
            (dmk_ref, own_dmk_ref, far_dmk_ref, mem_at),
            (dmv_ref, own_dmv_ref, far_dmv_ref, mem_at + width),
        ):
            own_low, far_low = low(ref[:own_mem, :]), low(ref[own_mem:, :])
            own[0] = ref[:own_mem, :]
            far[0] = far_low
            g_ref[:, at : at + width] += nn(turned[0], own_low) + nn(turned[1], far_low)

    @pl.when((micro == pl.num_programs(0) - 1) & (tile == pl.num_programs(1) - 1))
    def _():
        lane = lax.broadcasted_iota(jnp.int32, (width, LANES), 1)
        small = jnp.zeros((width, LANES), jnp.float32)
        for n in range(par_count):
            small = jnp.where(lane == n, jnp.sum(gpar_ref[n], axis=1, keepdims=True), small)
        for c in range(hidden // chunk):
            column = jnp.sum(gfb_ref[c * chunk : (c + 1) * chunk, :], axis=1, keepdims=True)
            small = jnp.where(lane == par_count + c, column, small)
        g_ref[:, mem_at + 2 * width :] = small
        slots, step = hidden // width, block
        copies = []
        for number, at in enumerate(range(0, g_ref.shape[1], step)):
            cols = min(step, g_ref.shape[1] - at)
            slot = number % slots
            if number >= slots:
                copies[number - slots].wait()
            spot = slice(slot * width, (slot + 1) * width)
            act_ref[spot, :cols] = low(g_ref[:, at : at + cols])
            copy = pltpu.make_async_copy(
                act_ref.at[spot, :cols], g_out_ref.at[:, at : at + cols], sems.at[slot]
            )
            copy.start()
            copies.append(copy)
        for copy in copies[-slots:]:
            copy.wait()


def middle(x, cot, self_out, memory, far_memory, rest, hidden, block=256):
    micro, rows, width = x.shape
    own_mem = memory.shape[1]
    mem_rows = 2 * own_mem
    f32, bf16 = jnp.float32, jnp.bfloat16
    row_block = pl.BlockSpec((1, block, width), lambda m, i: (m, i, 0))
    tall_block = pl.BlockSpec((1, width, block), lambda m, i: (m, 0, i))
    mem_block = pl.BlockSpec((1, own_mem, width), lambda m, i: (m, 0, 0))

    def fixed(columns, place):
        return pl.BlockSpec(
            (width, columns), lambda m, i: (0, place), pipeline_mode=pl.Buffered(1)
        )

    base = 2 * hidden // width
    columns = 2 * hidden + 5 * width + LANES
    mem_out = lambda kind: jax.ShapeDtypeStruct((micro, own_mem, width), kind)
    return pl.pallas_call(
        middle_kernel,
        out_shape=[
            jax.ShapeDtypeStruct((micro, rows, width), bf16),
            jax.ShapeDtypeStruct((micro, width, rows), bf16),
            jax.ShapeDtypeStruct((micro, HEADS, rows), f32),
            jax.ShapeDtypeStruct((micro, rows, width), f32),
            mem_out(f32),
            mem_out(f32),
            mem_out(bf16),
            mem_out(bf16),
        ]
        + [jax.ShapeDtypeStruct((width, columns), bf16)],
        grid=(micro, rows // block),
        in_specs=[row_block, row_block, tall_block, mem_block, mem_block]
        + [fixed(hidden, 0), fixed(hidden, 1)]
        + [fixed(width, base + n) for n in range(5)]
        + [fixed(LANES, (base + 5) * width // LANES)],
        out_specs=[
            row_block,
            tall_block,
            pl.BlockSpec((1, HEADS, block), lambda m, i: (m, 0, i)),
            row_block,
        ]
        + [mem_block] * 4
        + [pl.BlockSpec(memory_space=pl.ANY)],
        scratch_shapes=[
            pltpu.VMEM((mem_rows, width), bf16),
            pltpu.VMEM((mem_rows, width), bf16),
            pltpu.VMEM((width, mem_rows), bf16),
            pltpu.VMEM((width, mem_rows), bf16),
            pltpu.VMEM((hidden, width), bf16),
            pltpu.VMEM((width, hidden), bf16),
            pltpu.VMEM((width, width), bf16),
            pltpu.VMEM((width, width), bf16),
            pltpu.VMEM((width, width), bf16),
            pltpu.VMEM((12, width, LANES), bf16),
            pltpu.VMEM((hidden, LANES), bf16),
            pltpu.VMEM((mem_rows, width), f32),
            pltpu.VMEM((mem_rows, width), f32),
            pltpu.VMEM((12, width, LANES), f32),
            pltpu.VMEM((hidden, LANES), f32),
            pltpu.VMEM((HEADS, mem_rows, block), f32),
            pltpu.VMEM((hidden, block), bf16),
            pltpu.VMEM((hidden, block), f32),
            pltpu.VMEM((width, block), f32),
            pltpu.VMEM((hidden, block), bf16),
            pltpu.VMEM((width, columns), f32),
            pltpu.SemaphoreType.DMA((hidden // width,)),
        ],
        compiler_params=pltpu.CompilerParams(vmem_limit_bytes=61 << 20),
        cost_estimate=pl.CostEstimate(
            flops=6 * micro * rows * width * (3 * width + 2 * hidden + 4 * mem_rows),
            bytes_accessed=20 * micro * rows * width + 30 * width * (width + hidden),
            transcendentals=micro * rows * (HEADS * mem_rows + hidden),
        ),
        name="middle",
    )(x, cot, self_out, memory, far_memory, *[rest] * 8)


def input_grad_kernel(
    dqt_ref, dk_ref, dv_ref, far_dk_ref, far_dv_ref, w_ref, skip_ref, *others
):
    out_ref = others[-1]
    width = dk_ref.shape[2]
    dk = low(wide(dk_ref[0]) + wide(far_dk_ref[0]))
    dv = low(wide(dv_ref[0]) + wide(far_dv_ref[0]))
    out_ref[0] = low(
        nt(jnp.transpose(dqt_ref[0]), w_ref[:, :width])
        + nt(dk, w_ref[:, width : 2 * width])
        + nt(dv, w_ref[:, 2 * width :])
        + skip_ref[0]
    )


def input_gradient(first, count, dqt, dk, dv, far_dk, far_dv, w, skip, so_far=None, block=512):
    micro, rows, width = skip.shape
    row_block = pl.BlockSpec((1, block, width), lambda m, i: (first + m, i, 0))
    before = [] if so_far is None else [so_far]
    return pl.pallas_call(
        input_grad_kernel,
        out_shape=jax.ShapeDtypeStruct((micro, rows, width), jnp.bfloat16),
        grid=(count, rows // block),
        in_specs=[pl.BlockSpec((1, width, block), lambda m, i: (first + m, 0, i))]
        + [row_block] * 4
        + [
            pl.BlockSpec(w.shape, lambda m, i: (0, 0), pipeline_mode=pl.Buffered(1)),
            row_block,
        ]
        + [pl.BlockSpec(memory_space=pl.ANY)] * len(before),
        out_specs=row_block,
        input_output_aliases={7: 0} if before else {},
        compiler_params=pltpu.CompilerParams(vmem_limit_bytes=VMEM_LIMIT),
        cost_estimate=pl.CostEstimate(
            flops=6 * count * rows * width * width,
            bytes_accessed=16 * count * rows * width + 6 * width * width,
            transcendentals=0,
        ),
        name="input_gradient",
    )(dqt, dk, dv, far_dk, far_dv, w, skip, *before)


def total_tn(left, right):
    return tn(left.reshape(-1, left.shape[-1]), right.reshape(-1, right.shape[-1]))


def flat_nn(left, right):
    return nn(left.reshape(-1, left.shape[-1]), right).reshape(left.shape[:-1] + (right.shape[1],))


def flat_nt(left, right):
    return nt(left.reshape(-1, left.shape[-1]), right).reshape(left.shape[:-1] + (right.shape[0],))


def body(
    layer_in,
    memory,
    seg_ids,
    offsets,
    cotangent,
    attn_q,
    attn_k,
    attn_v,
    attn_o,
    w_in,
    w_out,
    ffn_bias,
    out_bias,
    omega,
    ln_gain,
    ln_bias,
):
    axis = "dp"
    is_prompt = lax.axis_index(axis) % 2 == 1
    own_rows = attn_q.shape[1]
    width = attn_q.shape[2]
    hidden = w_in.shape[1]
    mem_rows = memory.shape[1]

    packed = jnp.concatenate([attn_q[0], attn_k[0], attn_v[0]], axis=1)
    packed, w_in, w_out, small_parts, layer_in, memory = lax.optimization_barrier(
        (packed, w_in, w_out, (out_bias, omega, ln_gain, ln_bias, ffn_bias), layer_in, memory)
    )
    first = tree_gather(packed, axis)
    far_x = prompt_to_continuation(layer_in, axis)
    far_memory = from_partner(memory, axis, 0)
    parts = hidden // width
    small = jnp.concatenate(
        [p.T for p in small_parts[:4]] + [small_parts[4].reshape(own_rows, -1)], axis=1
    )
    small_cols = small.shape[1]
    rest = lax.all_gather(
        jnp.concatenate(
            [
                jnp.swapaxes(w_in.reshape(own_rows, width, parts), 1, 2).reshape(own_rows, -1),
                w_out.reshape(own_rows, -1),
                attn_o[0],
                attn_q[1],
                attn_o[1],
                attn_k[1],
                attn_v[1],
                jnp.pad(small, ((0, 0), (0, LANES - small_cols))),
            ],
            axis=1,
        ),
        axis,
        axis=0,
        tiled=True,
    )
    limits, tiles = mask_limits(seg_ids[:, 0], offsets[:, 0], is_prompt)
    qt, kv, kvt, far_kv, far_kvt = project(layer_in, far_x, first)
    self_out, lse = self_forward(qt, kv, kvt, far_kv, far_kvt, limits, tiles)
    (
        final,
        dso,
        delta,
        skip,
        own_mk,
        own_mv,
        far_mk,
        far_mv,
        g_main,
    ) = middle(layer_in, cotangent, self_out, memory, far_memory, rest, hidden)

    summed = lax.psum_scatter(g_main, axis, scatter_dimension=0, tiled=True)
    dqt, far_dk, far_dv, dk, dv, g_late = self_backward(
        qt, kv, kvt, far_kv, far_kvt, dso, lse, delta, limits, tiles, layer_in, far_x
    )
    far_dk, far_dv = continuation_to_prompt((far_dk, far_dv), axis)
    late = TreeScatter(g_late, axis)
    far_mk, far_mv = from_partner((far_mk, far_mv), axis, 0)
    far_mk = late.send(far_mk)
    mem_dk = low(own_mk + wide(far_mk))
    mem_dv = low(own_mv + wide(far_mv))
    at = 2 * hidden + 3 * width
    memory_grad = low(
        flat_nt(mem_dk, rest[:, at : at + width])
        + flat_nt(mem_dv, rest[:, at + width : at + 2 * width])
    )
    late.receive(memory_grad)
    input_grad = None
    micro = layer_in.shape[0]
    for begin, count in ((0, micro - 1), (micro - 1, 1)):
        skip = late.send(skip)
        input_grad = input_gradient(
            begin, count, dqt, dk, dv, far_dk, far_dv, first, skip, input_grad
        )
        late.receive(input_grad)
    s_c = late.finish()
    summed = wide(summed)
    s_q0, s_k0, s_v0 = (s_c[:, k * width : (k + 1) * width] for k in range(3))
    s_in = jnp.swapaxes(summed[:, :hidden].reshape(own_rows, parts, width), 1, 2)
    s_in = s_in.reshape(own_rows, hidden)
    s_out = summed[:, hidden : 2 * hidden].reshape(w_out.shape)
    s_o0, s_q1, s_o1, s_k1, s_v1 = (
        summed[:, 2 * hidden + k * width :][:, :width] for k in range(5)
    )
    s_small = summed[:, 2 * hidden + 5 * width :][:, :small_cols]
    return (
        final,
        input_grad,
        memory_grad,
        jnp.stack([s_q0, s_q1]),
        jnp.stack([s_k0, s_k1]),
        jnp.stack([s_v0, s_v1]),
        jnp.stack([s_o0, s_o1]),
        s_in,
        s_out,
        s_small[:, 12:].reshape(-1),
        s_small[:, 0:3].T,
        s_small[:, 3:6].T,
        s_small[:, 6:9].T,
        s_small[:, 9:12].T,
    )


def solution(mesh):
    rows = P(None, "dp", None)
    small = P(None, "dp")
    return jax.shard_map(
        body,
        mesh=mesh,
        in_specs=(rows,) * 9 + (P("dp", None), P("dp", None), P("dp"), small, small, small, small),
        out_specs=(rows,) * 7 + (P("dp", None), P("dp", None), P("dp"), small, small, small, small),
        check_vma=False,
    )
```

```python
import functools

import jax
import jax.numpy as jnp
from jax import lax
from jax.experimental import pallas as pl
from jax.experimental.pallas import tpu as pltpu
from jax.sharding import PartitionSpec as P

HEADS = 8
EPS = 1e-05
NEG = -1e30
LANES = 128
VMEM_LIMIT = 56 << 20


def nn(left, right):
    return lax.dot_general(
        left, right, (((1,), (0,)), ((), ())), preferred_element_type=jnp.float32
    )


def nt(left, right):
    return lax.dot_general(
        left, right, (((1,), (1,)), ((), ())), preferred_element_type=jnp.float32
    )


def tn(left, right):
    return lax.dot_general(
        left, right, (((0,), (0,)), ((), ())), preferred_element_type=jnp.float32
    )


def low(values):
    return values.astype(jnp.bfloat16)


def wide(values):
    return values.astype(jnp.float32)


def stages_of(axis):
    bits = (lax.axis_size(axis) - 1).bit_length()
    return [(0, 1)] + [(bit, min(2, bits - bit)) for bit in range(1, bits, 2)]


def from_partner(x, axis, bit):
    return lax.ppermute(x, axis, [(i, i ^ 1 << bit) for i in range(lax.axis_size(axis))])


def prompt_to_continuation(x, axis):
    return lax.ppermute(x, axis, [(i + 1, i) for i in range(0, lax.axis_size(axis), 2)])


def continuation_to_prompt(x, axis):
    return lax.ppermute(x, axis, [(i, i + 1) for i in range(0, lax.axis_size(axis), 2)])


def shifted(x, axis, offset):
    return lax.ppermute(x, axis, [(i, i ^ offset) for i in range(lax.axis_size(axis))])


def tree_gather(x, axis):
    stages = stages_of(axis)
    me = lax.axis_index(axis)
    block = x.reshape((1,) * len(stages) + x.shape)
    for number in reversed(range(len(stages))):
        bit, count = stages[number]
        dim = len(stages) - 1 - number
        place = (me >> bit) & ((1 << count) - 1)
        parts = [block] + [shifted(block, axis, k << bit) for k in range(1, 1 << count)]
        out = []
        for spot in range(1 << count):
            piece = parts[spot]
            for mine in range(1, 1 << count):
                piece = jnp.where(place == mine, parts[spot ^ mine], piece)
            out.append(piece)
        block = jnp.concatenate(out, dim)
    return block.reshape((-1,) + x.shape[1:])


class TreeScatter:
    def __init__(self, array, axis):
        self.axis = axis
        self.stages = stages_of(axis)
        self.me = lax.axis_index(axis)
        self.own = (array.shape[0] // lax.axis_size(axis),) + array.shape[1:]
        sizes = tuple(1 << count for _, count in reversed(self.stages))
        self.block = array.reshape(sizes + self.own)
        self.number = 0

    def send(self, after=None):
        bit, count = self.stages[self.number]
        dim = len(self.stages) - 1 - self.number
        place = (self.me >> bit) & ((1 << count) - 1)
        pick = lambda k: lax.dynamic_index_in_dim(self.block, place ^ k, dim, keepdims=True)
        aways = [low(pick(k)) for k in range(1, 1 << count)]
        if after is not None:
            after, aways = lax.optimization_barrier((after, aways))
        self.keep = pick(0)
        self.got = [shifted(a, self.axis, k << bit) for k, a in enumerate(aways, 1)]
        return after

    def receive(self, behind=None):
        if behind is not None:
            self.got, _ = lax.optimization_barrier((self.got, behind))
        self.block = sum([wide(g) for g in self.got], self.keep)
        self.number += 1

    def finish(self):
        while self.number < len(self.stages):
            self.send()
            self.receive()
        return self.block.reshape(self.own)


def tall_sum(values):
    return jnp.sum(values.reshape(-1, 8, values.shape[1]), axis=0)


def tall_max(values):
    return jnp.max(values.reshape(-1, 8, values.shape[1]), axis=0)


def alone(pair, number):
    half = pair.shape[0] // 2
    blank = jnp.zeros((half, pair.shape[1]), pair.dtype)
    if number == 0:
        return jnp.concatenate([pair[:half], blank], axis=0)
    return jnp.concatenate([blank, pair[half:]], axis=0)


def project_kernel(x_ref, far_ref, w_ref, qt_ref, kv_ref, kvt_ref, fkv_ref, fkvt_ref):
    width = x_ref.shape[2]
    for c in range(3):
        part = slice(c * width, (c + 1) * width)
        here = low(nn(x_ref[0], w_ref[:, part]))
        if c == 0:
            qt_ref[0] = jnp.transpose(here)
            continue
        into = slice((c - 1) * width, c * width)
        kv_ref[0, :, into] = here
        kvt_ref[0, into, :] = jnp.transpose(here)
        there = low(nn(far_ref[0], w_ref[:, part]))
        fkv_ref[0, :, into] = there
        fkvt_ref[0, into, :] = jnp.transpose(there)


def project(x, far, w, block=512):
    micro, rows, width = x.shape
    tall = lambda n: jax.ShapeDtypeStruct((micro, n, rows), jnp.bfloat16)
    long = jax.ShapeDtypeStruct((micro, rows, 2 * width), jnp.bfloat16)
    rows_in = pl.BlockSpec((1, block, width), lambda m, i: (m, i, 0))
    rows_out = pl.BlockSpec((1, block, 2 * width), lambda m, i: (m, i, 0))
    turned = lambda n: pl.BlockSpec((1, n, block), lambda m, i: (m, 0, i))
    return pl.pallas_call(
        project_kernel,
        out_shape=(tall(width), long, tall(2 * width), long, tall(2 * width)),
        grid=(micro, rows // block),
        in_specs=[
            rows_in,
            rows_in,
            pl.BlockSpec(w.shape, lambda m, i: (0, 0), pipeline_mode=pl.Buffered(1)),
        ],
        out_specs=[turned(width), rows_out, turned(2 * width), rows_out, turned(2 * width)],
        compiler_params=pltpu.CompilerParams(vmem_limit_bytes=VMEM_LIMIT),
        cost_estimate=pl.CostEstimate(
            flops=2 * 5 * micro * rows * width * width,
            bytes_accessed=22 * micro * rows * width,
            transcendentals=0,
        ),
        name="project",
    )(x, far, w)


def self_forward_kernel(
    tq, tk, pairs, tiles, qt_ref, kp_ref, kl_ref, vtp_ref, vtl_ref, lim_ref, ot_ref, lse_ref, s_ref, e_ref
):
    micro, tile = pl.program_id(0), pl.program_id(1)
    prefix_rows = kp_ref.shape[1]
    prefix_tiles = tiles[micro, tile, 0]
    local_first, local_end = tiles[micro, tile, 1], tiles[micro, tile, 2]
    reach, start = lim_ref[0, 0:1, :], lim_ref[0, 1:2, :]
    rows = tile * tq + lax.broadcasted_iota(jnp.int32, (1, tq), 1)
    key_at = lax.broadcasted_iota(jnp.int32, (tk, tq), 0)
    heads = 2 * pairs
    size = LANES // 2

    def prefix_mask(j):
        return key_at < reach - j * tk

    def local_mask(j):
        return (key_at <= rows - j * tk) & (key_at >= start - j * tk)

    ot_ref[0] = jnp.zeros((ot_ref.shape[1], tq), jnp.float32)
    for group in range(HEADS // heads):
        queries = []
        for h in range(heads):
            p = group * pairs + h // 2
            pair = qt_ref[0, p * LANES : (p + 1) * LANES, :] * jnp.bfloat16(0.125)
            queries.append(alone(pair, h % 2))

        def score(k_ref, offset, masker, j, tops):
            base = pl.multiple_of(j * tk, tk)
            seen = masker(j)
            out = []
            for h in range(heads):
                p = group * pairs + h // 2
                s = nn(k_ref[0, pl.ds(base, tk), p * LANES : (p + 1) * LANES], queries[h])
                s = jnp.where(seen, s, NEG)
                s_ref[h, pl.ds(pl.multiple_of(offset + base, tk), tk), :] = s
                out.append(jnp.maximum(tops[h], tall_max(s)))
            return tuple(out)

        tops = tuple(jnp.full((8, tq), NEG, jnp.float32) for _ in range(heads))
        tops = lax.fori_loop(
            0, prefix_tiles, functools.partial(score, kp_ref, 0, prefix_mask), tops
        )
        tops = lax.fori_loop(
            local_first,
            local_end,
            functools.partial(score, kl_ref, prefix_rows, local_mask),
            tops,
        )
        tops = [jnp.max(t, axis=0, keepdims=True) for t in tops]

        def mix(vt_ref, offset, j, carry):
            base = pl.multiple_of(j * tk, tk)
            out = []
            for h in range(heads):
                e = jnp.exp(
                    s_ref[h, pl.ds(pl.multiple_of(offset + base, tk), tk), :] - tops[h]
                )
                out.append(carry[h] + tall_sum(e))
                e_ref[h] = low(e)
            for h in range(heads):
                head = group * heads + h
                part = slice(head * size, (head + 1) * size)
                ot_ref[0, part, :] += nn(vt_ref[0, part, pl.ds(base, tk)], e_ref[h])
            return tuple(out)

        carry = (jnp.zeros((8, tq), jnp.float32),) * heads
        carry = lax.fori_loop(0, prefix_tiles, functools.partial(mix, vtp_ref, 0), carry)
        carry = lax.fori_loop(
            local_first, local_end, functools.partial(mix, vtl_ref, prefix_rows), carry
        )
        for h in range(heads):
            head = group * heads + h
            total = jnp.sum(carry[h], axis=0, keepdims=True)
            part = slice(head * size, (head + 1) * size)
            ot_ref[0, part, :] = ot_ref[0, part, :] / total
            lse_ref[0, head : head + 1, :] = tops[h] + jnp.log(total)


def self_forward(qt, kv, kvt, far_kv, far_kvt, limits, tiles, tq=256, tk=256, pairs=4):
    micro, width, rows = qt.shape
    return pl.pallas_call(
        functools.partial(self_forward_kernel, tq, tk, pairs),
        out_shape=(
            jax.ShapeDtypeStruct((micro, width, rows), jnp.float32),
            jax.ShapeDtypeStruct((micro, HEADS, rows), jnp.float32),
        ),
        grid_spec=pltpu.PrefetchScalarGridSpec(
            num_scalar_prefetch=1,
            grid=(micro, rows // tq),
            in_specs=[
                pl.BlockSpec((1, width, tq), lambda m, i, s: (m, 0, i)),
                pl.BlockSpec((1, rows, width), lambda m, i, s: (m, 0, 0)),
                pl.BlockSpec((1, rows, width), lambda m, i, s: (m, 0, 0)),
                pl.BlockSpec((1, width, rows), lambda m, i, s: (m, 1, 0)),
                pl.BlockSpec((1, width, rows), lambda m, i, s: (m, 1, 0)),
                pl.BlockSpec((1, 2, tq), lambda m, i, s: (m, 0, i)),
            ],
            out_specs=[
                pl.BlockSpec((1, width, tq), lambda m, i, s: (m, 0, i)),
                pl.BlockSpec((1, HEADS, tq), lambda m, i, s: (m, 0, i)),
            ],
            scratch_shapes=[
                pltpu.VMEM((2 * pairs, 2 * rows, tq), jnp.float32),
                pltpu.VMEM((2 * pairs, tk, tq), jnp.bfloat16),
            ],
        ),
        compiler_params=pltpu.CompilerParams(vmem_limit_bytes=VMEM_LIMIT),
        cost_estimate=pl.CostEstimate(
            flops=4 * micro * rows * rows * width,
            bytes_accessed=16 * micro * rows * width,
            transcendentals=micro * rows * rows * HEADS,
        ),
        name="self_forward",
    )(tiles, qt, far_kv, kv, far_kvt, kvt, limits)


def self_backward_kernel(
    tq,
    tk,
    pairs,
    tiles,
    qt_ref,
    kp_ref,
    vp_ref,
    kl_ref,
    vl_ref,
    ktp_ref,
    ktl_ref,
    dot_ref,
    lse_ref,
    delta_ref,
    lim_ref,
    x_ref,
    far_ref,
    w_ref,
    dqt_ref,
    away_ref,
    dkl_ref,
    dvl_ref,
    g_ref,
    sum_kp,
    sum_vp,
    sum_kl,
    sum_vl,
    sum_q,
    s_ref,
    dp_ref,
    p_ref,
    ds_ref,
):
    micro = pl.program_id(0)
    row_count = qt_ref.shape[2]
    size = LANES // 2

    @pl.when(micro == 0)
    def _():
        g_ref[...] = jnp.zeros_like(g_ref)

    for ref in (sum_kp, sum_vp, sum_kl, sum_vl):
        ref[...] = jnp.zeros_like(ref)
    key_at = lax.broadcasted_iota(jnp.int32, (tk, tq), 0)
    for i in range(row_count // tq):
        here = slice(i * tq, (i + 1) * tq)
        prefix_tiles = tiles[micro, i, 0]
        local_first, local_end = tiles[micro, i, 1], tiles[micro, i, 2]
        reach, start = lim_ref[0, 0:1, here], lim_ref[0, 1:2, here]
        rows = i * tq + lax.broadcasted_iota(jnp.int32, (1, tq), 1)
        queries, grads, totals, deltas = [], [], [], []
        for h in range(2 * pairs):
            part = slice(h // 2 * LANES, (h // 2 + 1) * LANES)
            queries.append(alone(qt_ref[0, part, here] * jnp.bfloat16(0.125), h % 2))
            grads.append(alone(dot_ref[0, part, here], h % 2))
            totals.append(lse_ref[0, 0, h : h + 1, here])
            deltas.append(delta_ref[0, 0, h : h + 1, here])
        sum_q[...] = jnp.zeros_like(sum_q)

        def body(k_ref, v_ref, kt_ref, sum_k, sum_v, masker, j, _):
            base = pl.multiple_of(j * tk, tk)
            seen = masker(j)
            heads = 2 * pairs
            cols = [slice(h // 2 * LANES, (h // 2 + 1) * LANES) for h in range(heads)]
            for h in range(heads):
                s_ref[h] = nn(k_ref[0, pl.ds(base, tk), cols[h]], queries[h])
                dp_ref[h] = nn(v_ref[0, pl.ds(base, tk), cols[h]], grads[h])
            for h in range(heads):
                p = jnp.exp(jnp.where(seen, s_ref[h], NEG) - totals[h])
                p_ref[h] = low(p)
                ds_ref[h] = low(p * (dp_ref[h] - deltas[h]))
            for h in range(heads):
                part = slice(h * size, (h + 1) * size)
                sum_v[pl.ds(base, tk), cols[h]] += nt(p_ref[h], grads[h])
                sum_k[pl.ds(base, tk), cols[h]] += nt(ds_ref[h], queries[h])
                sum_q[part, :] += nn(kt_ref[0, part, pl.ds(base, tk)], ds_ref[h])
            return 0

        def prefix_mask(j):
            return key_at < reach - j * tk

        def local_mask(j):
            return (key_at <= rows - j * tk) & (key_at >= start - j * tk)

        lax.fori_loop(
            0,
            prefix_tiles,
            functools.partial(body, kp_ref, vp_ref, ktp_ref, sum_kp, sum_vp, prefix_mask),
            0,
        )
        lax.fori_loop(
            local_first,
            local_end,
            functools.partial(body, kl_ref, vl_ref, ktl_ref, sum_kl, sum_vl, local_mask),
            0,
        )
        dqt_ref[0, :, here] = low(sum_q[...] * 0.125)
    dkp, dvp = low(sum_kp[...]), low(sum_vp[...])
    dkl_ref[0] = low(sum_kl[...])
    dvl_ref[0] = low(sum_vl[...])
    width = x_ref.shape[2]
    own, far = jnp.transpose(x_ref[0]), jnp.transpose(far_ref[0])
    g_ref[:, :width] += nt(own, dqt_ref[0])
    g_ref[:, width : 2 * width] += nn(own, dkl_ref[0]) + nn(far, dkp)
    g_ref[:, 2 * width :] += nn(own, dvl_ref[0]) + nn(far, dvp)
    away_ref[0] = low(nt(dkp, w_ref[:, :width]) + nt(dvp, w_ref[:, width:]))


def self_backward(
    qt, kv, kvt, far_kv, far_kvt, grad_out, lse, delta, limits, tiles, x, far_x, w_kv
):
    tq, tk, pairs = 256, 256, HEADS // 2
    micro, width, rows = qt.shape
    tall = pl.BlockSpec((1, width, rows), lambda m, s: (m, 0, 0))
    long = lambda place: pl.BlockSpec((1, rows, width), lambda m, s: (m, 0, place))
    line = pl.BlockSpec((1, 1, HEADS, rows), lambda m, s: (m, 0, 0, 0))
    bf16 = jax.ShapeDtypeStruct((micro, rows, width), jnp.bfloat16)
    return pl.pallas_call(
        functools.partial(self_backward_kernel, tq, tk, pairs),
        out_shape=(
            jax.ShapeDtypeStruct((micro, width, rows), jnp.bfloat16),
            bf16,
            bf16,
            bf16,
            jax.ShapeDtypeStruct((width, 3 * width), jnp.float32),
        ),
        grid_spec=pltpu.PrefetchScalarGridSpec(
            num_scalar_prefetch=1,
            grid=(micro,),
            in_specs=[
                tall,
                long(0),
                long(1),
                long(0),
                long(1),
                tall,
                tall,
                tall,
                line,
                line,
                pl.BlockSpec((1, 2, rows), lambda m, s: (m, 0, 0)),
                long(0),
                long(0),
                pl.BlockSpec(
                    (width, 2 * width), lambda m, s: (0, 0), pipeline_mode=pl.Buffered(1)
                ),
            ],
            out_specs=[tall]
            + [long(0)] * 3
            + [
                pl.BlockSpec(
                    (width, 3 * width), lambda m, s: (0, 0), pipeline_mode=pl.Buffered(1)
                )
            ],
            scratch_shapes=[pltpu.VMEM((rows, width), jnp.float32)] * 4
            + [pltpu.VMEM((width, tq), jnp.float32)]
            + [pltpu.VMEM((HEADS, tk, tq), t) for t in (jnp.float32, jnp.float32)]
            + [pltpu.VMEM((HEADS, tk, tq), t) for t in (jnp.bfloat16, jnp.bfloat16)],
        ),
        compiler_params=pltpu.CompilerParams(vmem_limit_bytes=60 << 20),
        cost_estimate=pl.CostEstimate(
            flops=10 * micro * rows * rows * width,
            bytes_accessed=40 * micro * rows * width,
            transcendentals=micro * rows * rows * HEADS,
        ),
        name="self_backward",
    )(
        tiles,
        qt,
        far_kv,
        far_kv,
        kv,
        kv,
        far_kvt,
        kvt,
        grad_out,
        lse[:, None],
        delta[:, None],
        limits,
        x,
        far_x,
        w_kv,
    )


def mask_limits(seg, off, is_prompt, tq=256, tk=256):
    micro, rows = seg.shape
    index = jnp.arange(off.shape[1], dtype=jnp.int32)
    own = seg[:, :, None] == index
    count = jnp.sum(own.astype(jnp.int32), axis=1)
    before = jnp.sum(jnp.where(index[:, None] > index[None, :], count[:, None, :], 0), axis=2)
    reach = jnp.sum(jnp.where(own, off[:, None, :], 0), axis=2)
    start = jnp.sum(jnp.where(own, before[:, None, :], 0), axis=2)
    reach = jnp.where(is_prompt, 0, reach)
    start = jnp.where(is_prompt, 0, start)
    tile_count = rows // tq
    most = jnp.max(reach.reshape(micro, tile_count, tq), axis=2)
    least = jnp.min(start.reshape(micro, tile_count, tq), axis=2)
    end = (jnp.arange(tile_count, dtype=jnp.int32) + 1) * tq
    tiles = jnp.stack(
        [
            (most + tk - 1) // tk,
            least // tk,
            jnp.broadcast_to((end + tk - 1) // tk, (micro, tile_count)),
        ],
        axis=2,
    )
    return jnp.stack([reach, start], axis=1), tiles


GELU_C = 0.7978845608028654
GELU_A = 0.044715


def spread(column, values):
    return jnp.concatenate([wide(column)] * (values.shape[1] // LANES), axis=1)


def lanes_of(values):
    total = values[:, :LANES]
    for c in range(1, values.shape[1] // LANES):
        total = total + values[:, c * LANES : (c + 1) * LANES]
    return total


def norm_tall(z):
    count = z.shape[0]
    mean = jnp.sum(tall_sum(z), axis=0, keepdims=True) / count
    centred = z - mean
    inv = lax.rsqrt(jnp.sum(tall_sum(centred * centred), axis=0, keepdims=True) / count + EPS)
    return centred * inv, inv


def norm_tall_backward(scaled, normed, inv):
    count = scaled.shape[0]
    mean = jnp.sum(tall_sum(scaled), axis=0, keepdims=True) / count
    slope = jnp.sum(tall_sum(scaled * normed), axis=0, keepdims=True) / count
    return inv * (scaled - mean - normed * slope)


def middle_kernel(
    x_ref,
    cot_ref,
    ot_ref,
    mem_ref,
    far_mem_ref,
    win_ref,
    wout_ref,
    wo0_ref,
    wq1_ref,
    wo1_ref,
    wk1_ref,
    wv1_ref,
    small_ref,
    out_ref,
    dso_ref,
    delta_ref,
    skip_ref,
    own_dmk_ref,
    own_dmv_ref,
    far_dmk_ref,
    far_dmv_ref,
    g_out_ref,
    mk_ref,
    mv_ref,
    mkt_ref,
    mvt_ref,
    wint_ref,
    woutt_ref,
    wo0t_ref,
    wq1t_ref,
    wo1t_ref,
    par_ref,
    fb_ref,
    dmk_ref,
    dmv_ref,
    gpar_ref,
    gfb_ref,
    p_ref,
    act_ref,
    slope_ref,
    mixed_ref,
    work_ref,
    g_ref,
    stage_ref,
    sems,
):
    micro, tile = pl.program_id(0), pl.program_id(1)
    width = x_ref.shape[2]
    hidden = win_ref.shape[1]
    mem_rows = mk_ref.shape[0]
    own_mem = mem_ref.shape[1]
    chunk = width
    half_mem = 256
    size = LANES // 2
    par_count = par_ref.shape[0]
    block = x_ref.shape[1]
    base = 2 * hidden
    mem_at = base + 3 * width

    @pl.when((micro == 0) & (tile == 0))
    def _():
        for ref in (g_ref, gpar_ref, gfb_ref):
            ref[...] = jnp.zeros_like(ref)
        for here, there in ((wo0_ref, wo0t_ref), (wq1_ref, wq1t_ref), (wo1_ref, wo1t_ref)):
            there[...] = jnp.transpose(here[...])
        for c in range(hidden // chunk):
            part = slice(c * chunk, (c + 1) * chunk)
            wint_ref[part, :] = jnp.transpose(win_ref[:, part])
            woutt_ref[:, part] = jnp.transpose(wout_ref[:, part])
            column = small_ref[:, par_count + c : par_count + c + 1]
            fb_ref[part, :] = low(jnp.broadcast_to(wide(column), (chunk, LANES)))
        for n in range(par_count):
            column = small_ref[:, n : n + 1]
            par_ref[n] = low(jnp.broadcast_to(wide(column), (width, LANES)))

    @pl.when(tile == 0)
    def _():
        dmk_ref[...] = jnp.zeros_like(dmk_ref)
        dmv_ref[...] = jnp.zeros_like(dmv_ref)
        for number, ref in enumerate((mem_ref, far_mem_ref)):
            part = slice(number * own_mem, (number + 1) * own_mem)
            for w_ref, m_ref, mt_ref in ((wk1_ref, mk_ref, mkt_ref), (wv1_ref, mv_ref, mvt_ref)):
                got = low(nn(ref[0], w_ref[...]))
                m_ref[part, :] = got
                mt_ref[:, part] = jnp.transpose(got)

    def par(kind, number, like):
        return spread(par_ref[3 * kind + number], like)

    def note(kind, number, values):
        gpar_ref[3 * kind + number] += lanes_of(values)

    x = wide(jnp.transpose(x_ref[0]))
    self_out = ot_ref[0]
    self_low = low(self_out)
    z = x * par(1, 0, x) + (nn(wo0t_ref[...], self_low) + par(0, 0, x))
    n1, inv1 = norm_tall(z)
    h1 = low(n1 * par(2, 0, x) + par(3, 0, x))
    cq = low(nn(wq1t_ref[...], h1)) * jnp.bfloat16(0.125)
    tops, shares = [], []
    for head in range(HEADS):
        pair = slice(head // 2 * LANES, (head // 2 + 1) * LANES)
        query = alone(cq[pair, :], head % 2)
        top = None
        for c in range(mem_rows // half_mem):
            keys = slice(c * half_mem, (c + 1) * half_mem)
            s = nn(mk_ref[keys, pair], query)
            p_ref[head, keys, :] = s
            here = tall_max(s)
            top = here if top is None else jnp.maximum(top, here)
        tops.append(jnp.max(top, axis=0, keepdims=True))
    for head in range(HEADS):
        part = slice(head * size, (head + 1) * size)
        total, mixed = 0.0, 0.0
        for c in range(mem_rows // half_mem):
            keys = slice(c * half_mem, (c + 1) * half_mem)
            e = jnp.exp(p_ref[head, keys, :] - tops[head])
            p_ref[head, keys, :] = e
            total = total + tall_sum(e)
            mixed = mixed + nn(mvt_ref[part, keys], low(e))
        share = 1.0 / jnp.sum(total, axis=0, keepdims=True)
        shares.append(share)
        mixed_ref[part, :] = mixed * share
    cross = low(mixed_ref[...])
    z = wide(h1) * par(1, 1, x) + (nn(wo1t_ref[...], cross) + par(0, 1, x))
    n2, inv2 = norm_tall(z)
    h2 = low(n2 * par(2, 1, x) + par(3, 1, x))
    for c in range(hidden // chunk):
        part = slice(c * chunk, (c + 1) * chunk)
        slope_ref[part, :] = nn(wint_ref[part, :], h2)
    for c in range(hidden // chunk):
        part = slice(c * chunk, (c + 1) * chunk)
        pre = slope_ref[part, :]
        pre = pre + spread(fb_ref[part, :], pre)
        square = pre * pre
        gate = 0.5 * jnp.tanh(pre * (square * (GELU_C * GELU_A) + GELU_C)) + 0.5
        act_ref[part, :] = low(pre * gate)
        slope_ref[part, :] = gate + (pre * (gate * (1.0 - gate))) * (
            square * (6.0 * GELU_C * GELU_A) + 2.0 * GELU_C
        )
    branch = nn(woutt_ref[...], act_ref[...])
    z = wide(h2) * par(1, 2, x) + (branch + par(0, 2, x))
    n3, inv3 = norm_tall(z)
    out_ref[0] = jnp.transpose(low(n3 * par(2, 2, x) + par(3, 2, x)))

    top = wide(jnp.transpose(cot_ref[0]))
    note(2, 2, top * n3)
    note(3, 2, top)
    dz = norm_tall_backward(top * par(2, 2, x), n3, inv3)
    note(1, 2, dz * wide(h2))
    df = low(dz)
    note(0, 2, wide(df))
    for c in range(hidden // chunk):
        part = slice(c * chunk, (c + 1) * chunk)
        work_ref[part, :] = low(nn(wout_ref[:, part], df))
    for c in range(hidden // chunk):
        part = slice(c * chunk, (c + 1) * chunk)
        dpre = low(wide(work_ref[part, :]) * slope_ref[part, :])
        gfb_ref[part, :] += lanes_of(wide(dpre))
        work_ref[part, :] = dpre
    dh = dz * par(1, 2, x) + nn(win_ref[...], work_ref[...])
    for c in range(hidden // chunk):
        part = slice(c * chunk, (c + 1) * chunk)
        at = hidden + c * chunk
        g_ref[:, at : at + chunk] += nt(act_ref[part, :], df)
        g_ref[:, part] += nt(h2, work_ref[part, :])
    note(2, 1, dh * n2)
    note(3, 1, dh)
    dz = norm_tall_backward(dh * par(2, 1, x), n2, inv2)
    note(1, 1, dz * wide(h1))
    dc = low(dz)
    note(0, 1, wide(dc))
    g_ref[:, base + 2 * width : base + 3 * width] += nt(cross, dc)
    dco = low(nn(wo1_ref[...], dc))
    queries = [alone(cq[h // 2 * LANES : (h // 2 + 1) * LANES], h % 2) for h in range(HEADS)]
    grads = [alone(dco[h // 2 * LANES : (h // 2 + 1) * LANES], h % 2) for h in range(HEADS)]
    weighed = wide(dco) * mixed_ref[...]
    deltas = [
        jnp.sum(tall_sum(weighed[h * size : (h + 1) * size]), axis=0, keepdims=True)
        for h in range(HEADS)
    ]
    mixed_ref[...] = jnp.zeros_like(mixed_ref)
    for c in range(mem_rows // half_mem):
        keys = slice(c * half_mem, (c + 1) * half_mem)
        spot = [slice(h * half_mem, (h + 1) * half_mem) for h in range(HEADS)]
        cols = [slice(h // 2 * LANES, (h // 2 + 1) * LANES) for h in range(HEADS)]
        for h in range(HEADS):
            slope_ref[spot[h], :] = nn(mv_ref[keys, cols[h]], grads[h])
        for h in range(HEADS):
            p = p_ref[h, keys, :] * shares[h]
            act_ref[spot[h], :] = low(p)
            work_ref[spot[h], :] = low(p * (slope_ref[spot[h], :] - deltas[h]))
        for h in range(HEADS):
            part = slice(h * size, (h + 1) * size)
            dmv_ref[keys, cols[h]] += nt(act_ref[spot[h], :], grads[h])
            dmk_ref[keys, cols[h]] += nt(work_ref[spot[h], :], queries[h])
            mixed_ref[part, :] += nn(mkt_ref[part, keys], work_ref[spot[h], :])
    dcq = low(mixed_ref[...] * 0.125)
    g_ref[:, base + width : base + 2 * width] += nt(h1, dcq)
    dh = nn(wq1_ref[...], dcq) + dz * par(1, 1, x)
    note(2, 0, dh * n1)
    note(3, 0, dh)
    dz = norm_tall_backward(dh * par(2, 0, x), n1, inv1)
    note(1, 0, dz * x)
    da = low(dz)
    note(0, 0, wide(da))
    g_ref[:, base : base + width] += nt(self_low, da)
    dso = low(nn(wo0_ref[...], da))
    dso_ref[0] = dso
    share = wide(dso) * self_out
    delta_ref[0] = jnp.concatenate(
        [
            jnp.sum(tall_sum(share[h * size : (h + 1) * size]), axis=0, keepdims=True)
            for h in range(HEADS)
        ],
        axis=0,
    )
    skip_ref[0] = jnp.transpose(dz * par(1, 0, x))

    @pl.when(tile == pl.num_programs(1) - 1)
    def _():
        turned = [jnp.transpose(mem_ref[0]), jnp.transpose(far_mem_ref[0])]
        for ref, own, far, at in (
            (dmk_ref, own_dmk_ref, far_dmk_ref, mem_at),
            (dmv_ref, own_dmv_ref, far_dmv_ref, mem_at + width),
        ):
            own_low, far_low = low(ref[:own_mem, :]), low(ref[own_mem:, :])
            own[0] = ref[:own_mem, :]
            far[0] = far_low
            g_ref[:, at : at + width] += nn(turned[0], own_low) + nn(turned[1], far_low)

    @pl.when((micro == pl.num_programs(0) - 1) & (tile == pl.num_programs(1) - 1))
    def _():
        lane = lax.broadcasted_iota(jnp.int32, (width, LANES), 1)
        small = jnp.zeros((width, LANES), jnp.float32)
        for n in range(par_count):
            small = jnp.where(lane == n, jnp.sum(gpar_ref[n], axis=1, keepdims=True), small)
        for c in range(hidden // chunk):
            column = jnp.sum(gfb_ref[c * chunk : (c + 1) * chunk, :], axis=1, keepdims=True)
            small = jnp.where(lane == par_count + c, column, small)
        g_ref[:, mem_at + 2 * width :] = small
        slots, step = stage_ref.shape[0], stage_ref.shape[2]
        copies = []
        for number, at in enumerate(range(0, g_ref.shape[1], step)):
            cols = min(step, g_ref.shape[1] - at)
            slot = number % slots
            if number >= slots:
                copies[number - slots].wait()
            stage_ref[slot, :, :cols] = low(g_ref[:, at : at + cols])
            copy = pltpu.make_async_copy(
                stage_ref.at[slot, :, :cols], g_out_ref.at[:, at : at + cols], sems.at[slot]
            )
            copy.start()
            copies.append(copy)
        for copy in copies[-slots:]:
            copy.wait()


def middle(x, cot, self_out, memory, far_memory, rest, hidden, block=256):
    micro, rows, width = x.shape
    own_mem = memory.shape[1]
    mem_rows = 2 * own_mem
    f32, bf16 = jnp.float32, jnp.bfloat16
    row_block = pl.BlockSpec((1, block, width), lambda m, i: (m, i, 0))
    tall_block = pl.BlockSpec((1, width, block), lambda m, i: (m, 0, i))
    mem_block = pl.BlockSpec((1, own_mem, width), lambda m, i: (m, 0, 0))

    def fixed(columns, place):
        return pl.BlockSpec(
            (width, columns), lambda m, i: (0, place), pipeline_mode=pl.Buffered(1)
        )

    base = 2 * hidden // width
    columns = 2 * hidden + 5 * width + LANES
    mem_out = lambda kind: jax.ShapeDtypeStruct((micro, own_mem, width), kind)
    return pl.pallas_call(
        middle_kernel,
        out_shape=[
            jax.ShapeDtypeStruct((micro, rows, width), bf16),
            jax.ShapeDtypeStruct((micro, width, rows), bf16),
            jax.ShapeDtypeStruct((micro, HEADS, rows), f32),
            jax.ShapeDtypeStruct((micro, rows, width), f32),
            mem_out(f32),
            mem_out(f32),
            mem_out(bf16),
            mem_out(bf16),
        ]
        + [jax.ShapeDtypeStruct((width, columns), bf16)],
        grid=(micro, rows // block),
        in_specs=[row_block, row_block, tall_block, mem_block, mem_block]
        + [fixed(hidden, 0), fixed(hidden, 1)]
        + [fixed(width, base + n) for n in range(5)]
        + [fixed(LANES, (base + 5) * width // LANES)],
        out_specs=[
            row_block,
            tall_block,
            pl.BlockSpec((1, HEADS, block), lambda m, i: (m, 0, i)),
            row_block,
        ]
        + [mem_block] * 4
        + [pl.BlockSpec(memory_space=pl.ANY)],
        scratch_shapes=[
            pltpu.VMEM((mem_rows, width), bf16),
            pltpu.VMEM((mem_rows, width), bf16),
            pltpu.VMEM((width, mem_rows), bf16),
            pltpu.VMEM((width, mem_rows), bf16),
            pltpu.VMEM((hidden, width), bf16),
            pltpu.VMEM((width, hidden), bf16),
            pltpu.VMEM((width, width), bf16),
            pltpu.VMEM((width, width), bf16),
            pltpu.VMEM((width, width), bf16),
            pltpu.VMEM((12, width, LANES), bf16),
            pltpu.VMEM((hidden, LANES), bf16),
            pltpu.VMEM((mem_rows, width), f32),
            pltpu.VMEM((mem_rows, width), f32),
            pltpu.VMEM((12, width, LANES), f32),
            pltpu.VMEM((hidden, LANES), f32),
            pltpu.VMEM((HEADS, mem_rows, block), f32),
            pltpu.VMEM((hidden, block), bf16),
            pltpu.VMEM((hidden, block), f32),
            pltpu.VMEM((width, block), f32),
            pltpu.VMEM((hidden, block), bf16),
            pltpu.VMEM((width, columns), f32),
            pltpu.VMEM((4, width, 256), bf16),
            pltpu.SemaphoreType.DMA((4,)),
        ],
        compiler_params=pltpu.CompilerParams(vmem_limit_bytes=62 << 20),
        cost_estimate=pl.CostEstimate(
            flops=6 * micro * rows * width * (3 * width + 2 * hidden + 4 * mem_rows),
            bytes_accessed=20 * micro * rows * width + 30 * width * (width + hidden),
            transcendentals=micro * rows * (HEADS * mem_rows + hidden),
        ),
        name="middle",
    )(x, cot, self_out, memory, far_memory, *[rest] * 8)


def input_grad_kernel(
    dqt_ref, dk_ref, dv_ref, far_ref, w_ref, skip_ref, *others
):
    out_ref = others[-1]
    width = dk_ref.shape[2]
    out_ref[0] = low(
        nt(jnp.transpose(dqt_ref[0]), w_ref[:, :width])
        + nt(dk_ref[0], w_ref[:, width : 2 * width])
        + nt(dv_ref[0], w_ref[:, 2 * width :])
        + wide(far_ref[0])
        + skip_ref[0]
    )


def input_gradient(first, count, dqt, dk, dv, far, w, skip, so_far=None, block=512):
    micro, rows, width = skip.shape
    row_block = pl.BlockSpec((1, block, width), lambda m, i: (first + m, i, 0))
    before = [] if so_far is None else [so_far]
    return pl.pallas_call(
        input_grad_kernel,
        out_shape=jax.ShapeDtypeStruct((micro, rows, width), jnp.bfloat16),
        grid=(count, rows // block),
        in_specs=[pl.BlockSpec((1, width, block), lambda m, i: (first + m, 0, i))]
        + [row_block] * 3
        + [
            pl.BlockSpec(w.shape, lambda m, i: (0, 0), pipeline_mode=pl.Buffered(1)),
            row_block,
        ]
        + [pl.BlockSpec(memory_space=pl.ANY)] * len(before),
        out_specs=row_block,
        input_output_aliases={6: 0} if before else {},
        compiler_params=pltpu.CompilerParams(vmem_limit_bytes=VMEM_LIMIT),
        cost_estimate=pl.CostEstimate(
            flops=6 * count * rows * width * width,
            bytes_accessed=16 * count * rows * width + 6 * width * width,
            transcendentals=0,
        ),
        name="input_gradient",
    )(dqt, dk, dv, far, w, skip, *before)


def total_tn(left, right):
    return tn(left.reshape(-1, left.shape[-1]), right.reshape(-1, right.shape[-1]))


def flat_nn(left, right):
    return nn(left.reshape(-1, left.shape[-1]), right).reshape(left.shape[:-1] + (right.shape[1],))


def flat_nt(left, right):
    return nt(left.reshape(-1, left.shape[-1]), right).reshape(left.shape[:-1] + (right.shape[0],))


def body(
    layer_in,
    memory,
    seg_ids,
    offsets,
    cotangent,
    attn_q,
    attn_k,
    attn_v,
    attn_o,
    w_in,
    w_out,
    ffn_bias,
    out_bias,
    omega,
    ln_gain,
    ln_bias,
):
    axis = "dp"
    is_prompt = lax.axis_index(axis) % 2 == 1
    own_rows = attn_q.shape[1]
    width = attn_q.shape[2]
    hidden = w_in.shape[1]
    mem_rows = memory.shape[1]

    packed = jnp.concatenate([attn_q[0], attn_k[0], attn_v[0]], axis=1)
    packed, w_in, w_out, small_parts, layer_in, memory = lax.optimization_barrier(
        (packed, w_in, w_out, (out_bias, omega, ln_gain, ln_bias, ffn_bias), layer_in, memory)
    )
    first = tree_gather(packed, axis)
    far_x = prompt_to_continuation(layer_in, axis)
    far_memory = from_partner(memory, axis, 0)
    parts = hidden // width
    small = jnp.concatenate(
        [jnp.concatenate(small_parts[:4]).T, small_parts[4].reshape(own_rows, -1)], axis=1
    )
    small_cols = small.shape[1]
    rest = lax.all_gather(
        jnp.concatenate(
            [
                jnp.swapaxes(w_in.reshape(own_rows, width, parts), 1, 2).reshape(own_rows, -1),
                w_out.reshape(own_rows, -1),
                attn_o[0],
                attn_q[1],
                attn_o[1],
                attn_k[1],
                attn_v[1],
                jnp.pad(small, ((0, 0), (0, LANES - small_cols))),
            ],
            axis=1,
        ),
        axis,
        axis=0,
        tiled=True,
    )
    limits, tiles = mask_limits(seg_ids[:, 0], offsets[:, 0], is_prompt)
    qt, kv, kvt, far_kv, far_kvt = project(layer_in, far_x, first)
    self_out, lse = self_forward(qt, kv, kvt, far_kv, far_kvt, limits, tiles)
    (
        final,
        dso,
        delta,
        skip,
        own_mk,
        own_mv,
        far_mk,
        far_mv,
        g_main,
    ) = middle(layer_in, cotangent, self_out, memory, far_memory, rest, hidden)

    summed = lax.psum_scatter(g_main, axis, scatter_dimension=0, tiled=True)
    dqt, away, dk, dv, g_late = self_backward(
        qt,
        kv,
        kvt,
        far_kv,
        far_kvt,
        dso,
        lse,
        delta,
        limits,
        tiles,
        layer_in,
        far_x,
        first[:, width:],
    )
    late = TreeScatter(g_late, axis)
    away = late.send(away)
    far = continuation_to_prompt(away, axis)
    late.receive()
    skip, far_mk, far_mv = late.send((skip, far_mk, far_mv))
    far_mk, far_mv = from_partner((far_mk, far_mv), axis, 0)
    micro = layer_in.shape[0]
    input_grad = input_gradient(0, micro - 1, dqt, dk, dv, far, first, skip)
    late.receive(input_grad)
    skip, far_mk, far_mv = late.send((skip, far_mk, far_mv))
    input_grad = input_gradient(micro - 1, 1, dqt, dk, dv, far, first, skip, input_grad)
    mem_dk = low(own_mk + wide(far_mk))
    mem_dv = low(own_mv + wide(far_mv))
    at = 2 * hidden + 3 * width
    memory_grad = low(
        flat_nt(mem_dk, rest[:, at : at + width])
        + flat_nt(mem_dv, rest[:, at + width : at + 2 * width])
    )
    summed = wide(summed)
    s_in = jnp.swapaxes(summed[:, :hidden].reshape(own_rows, parts, width), 1, 2)
    s_in = s_in.reshape(own_rows, hidden)
    s_out = summed[:, hidden : 2 * hidden].reshape(w_out.shape)
    s_o0, s_q1, s_o1, s_k1, s_v1 = (
        summed[:, 2 * hidden + k * width :][:, :width] for k in range(5)
    )
    s_small = summed[:, 2 * hidden + 5 * width :][:, :small_cols]
    late.receive((input_grad, memory_grad, s_in, s_out, s_small))
    s_c = late.finish()
    s_q0, s_k0, s_v0 = (s_c[:, k * width : (k + 1) * width] for k in range(3))
    return (
        final,
        input_grad,
        memory_grad,
        jnp.stack([s_q0, s_q1]),
        jnp.stack([s_k0, s_k1]),
        jnp.stack([s_v0, s_v1]),
        jnp.stack([s_o0, s_o1]),
        s_in,
        s_out,
        s_small[:, 12:].reshape(-1),
        s_small[:, 0:3].T,
        s_small[:, 3:6].T,
        s_small[:, 6:9].T,
        s_small[:, 9:12].T,
    )


def solution(mesh):
    rows = P(None, "dp", None)
    small = P(None, "dp")
    return jax.shard_map(
        body,
        mesh=mesh,
        in_specs=(rows,) * 9 + (P("dp", None), P("dp", None), P("dp"), small, small, small, small),
        out_specs=(rows,) * 7 + (P("dp", None), P("dp", None), P("dp"), small, small, small, small),
        check_vma=False,
    )
```
